256 devices in a mesh: tm: 64 (over y, x, z_lo, core), inp: 4 (over z_hi).
Axes of the slice: x: 4, y: 4, z: 8 (z_hi: 4, z_lo: 2; z = z_hi * 2 + z_lo), core: 2. Of those that a mesh axis runs over, the one named last changes fastest.
Arguments:
- voltages: bfloat16 [1024, 262144], P('inp', 'tm'), may hold values from -6 to 6
- input_gain: float32 [1024], P('inp'), may hold values from 0.5 to 2
- input_feed: int32 [1024], replicated, may hold values from 0 to 511
- beam_grid: int32 [1024], replicated, may hold values from 0 to 511
Outputs:
- visibilities: bfloat16 [512, 2, 1024, 1024], P(('tm', 'inp'))
- beam_power: float32 [512, 1024], P(('tm', 'inp'))
The draws below stay inside these ranges and needn't reach their ends.
All inputs are finite; a program needn't handle non-finite values.
Results may differ from the reference program's by a relative error of at most 0.0034.
Values may be sent and summed in bfloat16 or wider, within the bound.
A program may use at most 64 MiB of HBM per device.

```python
import math
import jax
import jax.numpy as jnp
from jax import lax

INPUTS = 1024
L = 1024
CH = 512
BEAMS = 1024
TAPS = 4
GRID = 512
FRAMES = 256
SAMPLES = 262144


def draw_voltages(key, part):
    noise_key = jax.random.fold_in(key, 11)
    sky_key = jax.random.fold_in(key, 12)
    noise_part = jax.random.normal(noise_key, (INPUTS, SAMPLES), jnp.float32)
    common = jax.random.normal(sky_key, (1, SAMPLES), jnp.float32)
    return jnp.clip(0.6 * (noise_part + common), -6.0, 6.0).astype(jnp.bfloat16)


def place_ends(entries, key, smallest, top_value):
    place = [jax.random.randint(jax.random.fold_in(key, axis), (), 0, length) for axis, length in enumerate(entries.shape)]
    main_axis = entries.shape.index(max(entries.shape))
    neighbour = place[:main_axis] + [(place[main_axis] + 1) % entries.shape[main_axis]] + place[main_axis + 1:]
    return entries.at[tuple(place)].set(smallest).at[tuple(neighbour)].set(top_value)


def shard_levels(own_key, extent, shards, least, largest):
    def one(dim, parts):
        steps = jax.random.uniform(jax.random.fold_in(jax.random.fold_in(own_key, 6), dim), (parts,), jnp.float32, least / len(shards), largest / len(shards))
        return jnp.repeat(jnp.exp(steps), extent[dim] // parts).reshape((-1,) + (1,) * (len(extent) - dim - 1))

    gain = one(*shards[0])
    for cut in shards[1:]:
        gain = gain * one(*cut)
    return gain


def setup_inputs(seed: int = 0) -> dict:
    key_of = jax.random.split(jax.random.key(seed), 5)
    voltages = draw_voltages(jax.random.fold_in(key_of[4], 71), 0)
    input_gain = jnp.clip(jnp.exp(math.log(2.0) - 1.3862944 * jax.random.uniform(key_of[1], (INPUTS,), jnp.float32) ** shard_levels(key_of[1], (INPUTS,), ((0, 4),), -0.2, 0.2)), 0.5, 2.0)
    input_feed = place_ends(jax.random.randint(key_of[2], (INPUTS,), 0, GRID), jax.random.fold_in(key_of[2], 1), 0, GRID - 1).astype(jnp.int32)
    beam_grid = place_ends(jax.random.randint(key_of[3], (BEAMS,), 0, GRID), jax.random.fold_in(key_of[3], 1), 0, GRID - 1).astype(jnp.int32)
    return dict(voltages=voltages, input_gain=input_gain, input_feed=input_feed, beam_grid=beam_grid)


def window_table():
    span = TAPS * L
    sample_pos = jnp.arange(span).astype(jnp.float32)
    sinc_part = jnp.sinc((sample_pos - span / 2) / L)
    hann_part = 0.5 - 0.5 * jnp.cos(2.0 * jnp.pi * sample_pos / span)
    return (sinc_part * hann_part).reshape(TAPS, L)

def dft_table(channel):
    lag_index = jnp.arange(L).astype(jnp.int32)
    phase_step = lag_index[:, None] * channel[None, :] % L
    radians = 2.0 * jnp.pi * phase_step.astype(jnp.float32) / L
    factor = 1.0 / math.sqrt(L)
    stacked = jnp.stack([jnp.cos(radians), -jnp.sin(radians)], 2) * factor
    return stacked.astype(jnp.bfloat16).reshape(L, 2 * channel.shape[0])

def steer_table(input_feed, beam_grid):
    input_count = input_feed.shape[0]
    phase_step = input_feed[:, None] * beam_grid[None, :] % GRID
    radians = 2.0 * jnp.pi * phase_step.astype(jnp.float32) / GRID
    factor = 1.0 / math.sqrt(input_count)
    cosine = jnp.cos(radians) * factor
    sine_part = jnp.sin(radians) * factor
    top_rows = jnp.concatenate([cosine, sine_part], 1)
    low_rows = jnp.concatenate([-sine_part, cosine], 1)
    return jnp.concatenate([top_rows, low_rows], 0).astype(jnp.bfloat16)

def channel_products(spectrum, steer):
    real_part = spectrum[0]
    imag_part = spectrum[1]
    input_count = real_part.shape[0]
    frame_total = real_part.shape[1]
    stacked = jnp.concatenate([real_part, imag_part], 1)
    rotated = jnp.concatenate([imag_part, -real_part], 1)
    both = jnp.concatenate([stacked, rotated], 0)
    products = lax.dot_general(both, stacked, (((1,), (1,)), ((), ())), preferred_element_type=jnp.float32)
    visible = (products / frame_total).reshape(2, input_count, input_count).astype(jnp.bfloat16)
    flat = spectrum.reshape(2 * input_count, frame_total)
    beams = lax.dot_general(steer, flat, (((0,), (0,)), ((), ())), preferred_element_type=jnp.float32)
    beam_count = beams.shape[0] // 2
    power = lax.optimization_barrier(jnp.mean(beams[:beam_count] ** 2 + beams[beam_count:] ** 2, axis=1))
    return (visible, power)

def reference(voltages, input_gain, input_feed, beam_grid):
    per_block = 16
    window = window_table()
    table = dft_table(jnp.arange(CH).astype(jnp.int32))
    padded = jnp.concatenate([voltages, jnp.zeros((INPUTS, (TAPS - 1) * L), jnp.bfloat16)], 1)

    def one_block(items):
        block_rows, gains = items
        summed = jnp.zeros((per_block, FRAMES, L), jnp.float32)
        for tap in range(TAPS):
            piece = block_rows[:, tap * L:tap * L + FRAMES * L].reshape(per_block, FRAMES, L)
            summed = summed + piece.astype(jnp.float32) * window[tap]
        filtered = (summed * gains[:, None, None]).astype(jnp.bfloat16)
        spectra = jnp.dot(filtered.reshape(per_block * FRAMES, L), table, preferred_element_type=jnp.float32)
        return spectra.astype(jnp.bfloat16).reshape(per_block, FRAMES, CH, 2)
    spectra = lax.map(one_block, (padded.reshape(INPUTS // per_block, per_block, padded.shape[1]), input_gain.reshape(INPUTS // per_block, per_block)))
    spectra = spectra.reshape(INPUTS, FRAMES, CH, 2).transpose(2, 3, 0, 1)
    steer = steer_table(input_feed, beam_grid)
    visible, power = lax.map(lambda spectrum: channel_products(spectrum, steer), spectra)
    return (visible, power)
```

```python
import functools
import math

import jax
import jax.numpy as jnp
import numpy as np
from jax import lax
from jax.experimental import pallas as pl
from jax.experimental.pallas import tpu as pltpu
from jax.sharding import PartitionSpec as P

MESH = pl.DeviceIdType.MESH
L = 1024
CH = 512
TAPS = 4
GRID = 512
LANES = 128


def window_table():
    span = TAPS * L
    pos = np.arange(span).astype(np.float64)
    sinc_part = np.sinc((pos - span / 2) / L)
    hann_part = 0.5 - 0.5 * np.cos(2.0 * np.pi * pos / span)
    return (sinc_part * hann_part).reshape(TAPS, L).astype(np.float32)


def dft_table():
    step = np.arange(CH)[:, None] * np.arange(L)[None, :] % L
    radians = 2.0 * np.pi * step / L
    rows = np.stack([np.cos(radians), -np.sin(radians)], 1) / math.sqrt(L)
    return rows.reshape(2 * CH, L).astype(jnp.bfloat16)


def steer_tables(input_feed, beam_grid):
    phase = (input_feed[:, None] * beam_grid[None, :]) & (GRID - 1)
    turned = phase + GRID // 8
    quarter = (turned >> 7) & 3
    rest = (turned & 127) - GRID // 8
    x = rest.astype(jnp.float32) * (2.0 * math.pi / GRID)
    y = x * x
    sine = x * (1.0 + y * (-1.0 / 6 + y * (1.0 / 120 + y * (-1.0 / 5040 + y * (1.0 / 362880)))))
    cosine = 1.0 + y * (-0.5 + y * (1.0 / 24 + y * (-1.0 / 720 + y * (1.0 / 40320))))
    swap = (quarter & 1) == 1
    factor = 1.0 / math.sqrt(input_feed.shape[0])
    c_sign = jnp.where((quarter == 1) | (quarter == 2), -factor, factor)
    s_sign = jnp.where(quarter >= 2, factor, -factor)
    c = jnp.where(swap, sine, cosine) * c_sign
    s = jnp.where(swap, cosine, sine) * s_sign
    return c.astype(jnp.bfloat16), s.astype(jnp.bfloat16)


def exchange_kernel(n_time, n_inp, volt, halo, gain, window, table, recv, filt, wide, send, s_sem, r_sem, l_sem):
    total = n_time * n_inp
    rows = volt.shape[0]
    frames = volt.shape[1] // L
    chunks = rows // LANES
    tm = lax.axis_index("tm")
    inp = lax.axis_index("inp")
    me = tm * n_inp + inp

    barrier = pltpu.get_barrier_semaphore()

    def greet(s, carry):
        d = lax.rem(me + s, total)
        pl.semaphore_signal(barrier, inc=1, device_id={"tm": d // n_inp, "inp": lax.rem(d, n_inp)}, device_id_type=MESH)
        return carry

    lax.fori_loop(1, total, greet, 0)
    last = tm == n_time - 1
    step_rows = 16
    for c in range(chunks):
        for f in range(frames):

            def one(i, carry):
                at = pl.multiple_of(i * step_rows, step_rows)
                from_rows = pl.ds(c * LANES + at, step_rows)
                summed = None
                for tap in range(TAPS):
                    g = f + tap
                    if g < frames:
                        piece = volt[from_rows, g * L : (g + 1) * L].astype(jnp.float32)
                    else:
                        piece = halo[from_rows, (g - frames) * L : (g - frames + 1) * L].astype(jnp.float32)
                        piece = jnp.where(last, 0.0, piece)
                    term = piece * window[tap : tap + 1, :]
                    summed = term if summed is None else summed + term
                filt[pl.ds(f * LANES + at, step_rows), :] = (summed * gain[from_rows, :]).astype(jnp.bfloat16)
                return carry

            lax.fori_loop(0, LANES // step_rows, one, 0)
        block = 256
        for b in range(2 * CH // block):
            part = lax.dot_general(
                table[b * block : (b + 1) * block, :],
                filt[...],
                (((1,), (1,)), ((), ())),
                preferred_element_type=jnp.float32,
            )
            for f in range(frames):
                wide[pl.ds(f, block, stride=frames), :] = part[:, f * LANES : (f + 1) * LANES]
            n = block * frames // 16
            send[c * total + b * n : c * total + (b + 1) * n] = wide[...].astype(jnp.bfloat16).reshape(n, 16, LANES)
        if c == 0:
            pl.semaphore_wait(barrier, total - 1)
        slot = (inp * chunks + c) * n_time + tm

        def ship(s, carry):
            d = lax.rem(me + s, total)
            pltpu.make_async_remote_copy(
                send.at[c * total + d],
                recv.at[slot],
                s_sem,
                r_sem,
                device_id={"tm": d // n_inp, "inp": lax.rem(d, n_inp)},
                device_id_type=MESH,
            ).start()
            return carry

        lax.fori_loop(1, total, ship, 0)
        pltpu.make_async_copy(send.at[c * total + me], recv.at[slot], l_sem.at[c]).start()
    for c in range(chunks):
        slot = (inp * chunks + c) * n_time + tm
        pltpu.make_async_copy(send.at[c * total + me], recv.at[slot], l_sem.at[c]).wait()
    everything = pl.ds(0, chunks * (total - 1))
    pltpu.make_async_copy(send.at[everything], send.at[everything], s_sem).wait()
    pltpu.make_async_copy(recv.at[everything], recv.at[everything], r_sem).wait()


def exchange(volt, halo, gain, n_time, n_inp):
    rows = volt.shape[0]
    frames = volt.shape[1] // L
    chunks = rows // LANES
    blocks = chunks * n_time * n_inp
    vmem = pl.BlockSpec(memory_space=pltpu.VMEM)
    return pl.pallas_call(
        functools.partial(exchange_kernel, n_time, n_inp),
        name="exchange",
        out_shape=jax.ShapeDtypeStruct((blocks, 16, LANES), jnp.bfloat16),
        in_specs=[vmem] * 5,
        out_specs=vmem,
        scratch_shapes=[
            pltpu.VMEM((frames * LANES, L), jnp.bfloat16),
            pltpu.VMEM((256 * frames, LANES), jnp.float32),
            pltpu.VMEM((blocks, 16, LANES), jnp.bfloat16),
            pltpu.SemaphoreType.DMA,
            pltpu.SemaphoreType.DMA,
            pltpu.SemaphoreType.DMA((chunks,)),
        ],
        compiler_params=pltpu.CompilerParams(collective_id=0, has_side_effects=True, vmem_limit_bytes=40 << 20),
    )(volt, halo, gain, jnp.asarray(window_table()), jnp.asarray(dft_table()))


def products_kernel(groups, n_time, recv, cosine, sine, visible, power, spec, turn, spec_t, turn_t):
    j = pl.program_id(1)
    ch = pl.program_id(0)
    depth = n_time * 8

    @pl.when(j == 0)
    def _():
        sign = jnp.where(lax.broadcasted_iota(jnp.int32, (depth, LANES), 0) % 8 < 4, 1.0, -1.0)
        for g in range(groups):
            part = recv[g * n_time : (g + 1) * n_time, pl.ds(pl.multiple_of(ch * 8, 8), 8), :].reshape(depth, LANES)
            wide = part.astype(jnp.float32)
            swapped = pltpu.roll(wide.reshape(n_time, 8, LANES), 4, 1).reshape(depth, LANES) * sign
            lanes = slice(g * LANES, (g + 1) * LANES)
            spec[:, lanes] = part
            turn[:, lanes] = swapped.astype(jnp.bfloat16)
            spec_t[lanes, :] = wide.T.astype(jnp.bfloat16)
            turn_t[lanes, :] = swapped.T.astype(jnp.bfloat16)

    width = visible.shape[-1]
    cols = pl.ds(pl.multiple_of(j * width, width), width)
    right = spec[:, cols]
    scale = 2.0 / depth
    visible[0, 0] = (jnp.dot(spec_t[...], right, preferred_element_type=jnp.float32) * scale).astype(jnp.bfloat16)
    visible[0, 1] = (jnp.dot(turn_t[...], right, preferred_element_type=jnp.float32) * scale).astype(jnp.bfloat16)
    beams = jnp.dot(spec[...], cosine[:, cols], preferred_element_type=jnp.float32) + jnp.dot(
        turn[...], sine[:, cols], preferred_element_type=jnp.float32
    )
    power[0] = jnp.sum(beams * beams, axis=0, keepdims=True) * scale


def products(recv, cosine, sine, n_time):
    groups = recv.shape[0] // n_time
    inputs, beams = cosine.shape
    width = 256
    depth = n_time * 8
    vmem = pl.BlockSpec(memory_space=pltpu.VMEM)
    visible, power = pl.pallas_call(
        functools.partial(products_kernel, groups, n_time),
        name="products",
        grid=(2, inputs // width),
        out_shape=(
            jax.ShapeDtypeStruct((2, 2, inputs, inputs), jnp.bfloat16),
            jax.ShapeDtypeStruct((2, 1, beams), jnp.float32),
        ),
        in_specs=[vmem] * 3,
        out_specs=(
            pl.BlockSpec((1, 2, inputs, width), lambda c, j: (c, 0, 0, j)),
            pl.BlockSpec((1, 1, width), lambda c, j: (c, 0, j)),
        ),
        scratch_shapes=[
            pltpu.VMEM((depth, inputs), jnp.bfloat16),
            pltpu.VMEM((depth, inputs), jnp.bfloat16),
            pltpu.VMEM((inputs, depth), jnp.bfloat16),
            pltpu.VMEM((inputs, depth), jnp.bfloat16),
        ],
        compiler_params=pltpu.CompilerParams(vmem_limit_bytes=40 << 20),
    )(recv, cosine, sine)
    return visible, power.reshape(2, beams)


def on_device(voltages, input_gain, input_feed, beam_grid):
    n_time = lax.axis_size("tm")
    n_inp = lax.axis_size("inp")
    route = [(i + 1, i) for i in range(n_time - 1)]
    halo = lax.ppermute(voltages[:, : (TAPS - 1) * L], "tm", route)
    cosine, sine = steer_tables(input_feed, beam_grid)
    recv = exchange(voltages, halo, input_gain[:, None], n_time, n_inp)
    return products(recv, cosine, sine, n_time)


def solution(mesh):
    return jax.shard_map(
        on_device,
        mesh=mesh,
        in_specs=(P("inp", "tm"), P("inp"), P(), P()),
        out_specs=(P(("tm", "inp"), None, None, None), P(("tm", "inp"), None)),
        check_vma=False,
    )
```

```python
import functools
import math

import jax
import jax.numpy as jnp
import numpy as np
from jax import lax
from jax.experimental import pallas as pl
from jax.experimental.pallas import tpu as pltpu
from jax.sharding import PartitionSpec as P

LOGICAL = pl.DeviceIdType.LOGICAL
L = 1024
CH = 512
TAPS = 4
GRID = 512
LANES = 128
PAIR = 2


def window_table():
    span = TAPS * L
    pos = np.arange(span).astype(np.float64)
    sinc_part = np.sinc((pos - span / 2) / L)
    hann_part = 0.5 - 0.5 * np.cos(2.0 * np.pi * pos / span)
    return (sinc_part * hann_part).reshape(TAPS, L).astype(np.float32)


def dft_table():
    step = np.arange(CH)[:, None] * np.arange(L)[None, :] % L
    radians = 2.0 * np.pi * step / L
    rows = np.stack([np.cos(radians), -np.sin(radians)], 1) / math.sqrt(L)
    return rows.reshape(2 * CH, L).astype(jnp.bfloat16)


def steer_block(phase, factor):
    phase = phase & (GRID - 1)
    turned = phase + GRID // 8
    quarter = (turned >> 7) & 3
    rest = (turned & 127) - GRID // 8
    x = rest.astype(jnp.float32) * (2.0 * math.pi / GRID)
    y = x * x
    sine = x * (1.0 + y * (-1.0 / 6 + y * (1.0 / 120 + y * (-1.0 / 5040 + y * (1.0 / 362880)))))
    cosine = 1.0 + y * (-0.5 + y * (1.0 / 24 + y * (-1.0 / 720 + y * (1.0 / 40320))))
    swap = (quarter & 1) == 1
    c_sign = jnp.where((quarter == 1) | (quarter == 2), -factor, factor)
    s_sign = jnp.where(quarter >= 2, factor, -factor)
    c = jnp.where(swap, sine, cosine) * c_sign
    s = jnp.where(swap, cosine, sine) * s_sign
    return c.astype(jnp.bfloat16), s.astype(jnp.bfloat16)


def arrange(recv, first, n_time, n_inp, spec, turn, spec_t, turn_t):
    width = recv.shape[2]
    half = n_time // 2
    rows = half * 8
    row = lax.broadcasted_iota(jnp.int32, (half, 8, width), 1)
    low = row < 4
    real = (row & 2) == 0
    for g in range(n_inp):
        lanes = slice(g * width, (g + 1) * width)
        got = recv[first + g * n_time : first + (g + 1) * n_time].astype(jnp.float32).reshape(half, 2, 8, width)
        even, odd = got[:, 0], got[:, 1]
        for ch in range(2):
            if ch == 0:
                y = jnp.where(low, even, pltpu.roll(odd, 4, 1))
            else:
                y = jnp.where(low, pltpu.roll(even, 4, 1), odd)
            z = jnp.where(real, pltpu.roll(y, 6, 1), -pltpu.roll(y, 2, 1))
            y = y.reshape(rows, width)
            z = z.reshape(rows, width)
            spec[ch, :, lanes] = y.astype(jnp.bfloat16)
            turn[ch, :, lanes] = z.astype(jnp.bfloat16)
            spec_t[ch, lanes, :] = y.T.astype(jnp.bfloat16)
            turn_t[ch, lanes, :] = z.T.astype(jnp.bfloat16)


def beam_sum(spec, turn, cosine, sine, ch, cols):
    beams = jnp.dot(spec[ch], cosine[:, cols], preferred_element_type=jnp.float32) + jnp.dot(
        turn[ch], sine[:, cols], preferred_element_type=jnp.float32
    )
    return jnp.sum(beams * beams, axis=0, keepdims=True)


def exchange_kernel(
    n_time,
    n_inp,
    volt,
    gain,
    window,
    table,
    feed,
    grid,
    recv,
    cosine,
    sine,
    sums,
    power,
    filt,
    wide,
    send,
    halo,
    gain_b,
    feed_b,
    spec,
    turn,
    spec_t,
    turn_t,
    s_sem,
    r_sem,
    hs_sem,
    hr_sem,
    l_sem,
):
    total = n_time * n_inp
    rows = volt.shape[0]
    inputs = feed.shape[1]
    frames = volt.shape[1] // L
    chunks = frames // PAIR
    tm = lax.axis_index("tm")
    inp = lax.axis_index("inp")
    me = tm * n_inp + inp
    barrier = pltpu.get_barrier_semaphore()

    def others(visit):
        def one(d, carry):
            visit(d)
            return carry

        lax.fori_loop(me + 1, total, one, 0)
        lax.fori_loop(0, me, one, 0)

    others(lambda d: pl.semaphore_signal(barrier, inc=1, device_id=d, device_id_type=LOGICAL))

    step_rows = 16

    def filter_frame(f):
        def one(i, carry):
            at = pl.ds(pl.multiple_of(i * step_rows, step_rows), step_rows)
            summed = None
            for tap in range(TAPS):
                g = f + tap
                if g < frames:
                    piece = volt[at, g * L : (g + 1) * L].astype(jnp.float32)
                else:
                    piece = halo[at, (g - frames) * L : (g - frames + 1) * L].astype(jnp.float32)
                term = piece * window[tap : tap + 1, :]
                summed = term if summed is None else summed + term
            scale = jnp.concatenate([gain_b[at, :]] * (L // LANES), 1)
            filt[at, :] = (summed * scale).astype(jnp.bfloat16)
            return carry

        lax.fori_loop(0, rows // step_rows, one, 0)

    def transform_frame(f):
        c, place = f // PAIR, f % PAIR
        block = 256
        for b in range(2 * CH // block):
            part = lax.dot_general(
                table[b * block : (b + 1) * block, :],
                filt[...],
                (((1,), (1,)), ((), ())),
                preferred_element_type=jnp.float32,
            )
            start = b * block * PAIR
            for h in range(rows // LANES):
                wide[h, pl.ds(start + place, block, stride=PAIR), :] = part[:, h * LANES : (h + 1) * LANES]
            if place == PAIR - 1:
                n = block * PAIR // 8
                for h in range(rows // LANES):
                    ready = wide[h, start : start + block * PAIR, :].astype(jnp.bfloat16).reshape(n, 8, LANES)
                    send[c * total + b * n : c * total + (b + 1) * n, :, h * LANES : (h + 1) * LANES] = ready

    def ship(c):
        slot = c * total + inp * n_time + tm

        def one(d):
            pltpu.make_async_remote_copy(
                send.at[c * total + d],
                recv.at[slot],
                s_sem.at[c],
                r_sem.at[c],
                device_id=d,
                device_id_type=LOGICAL,
            ).start()

        others(one)
        pltpu.make_async_copy(send.at[c * total + me], recv.at[slot], l_sem.at[c]).start()

    def arrived(c):
        slot = c * total + inp * n_time + tm
        pltpu.make_async_copy(send.at[c * total + me], recv.at[slot], l_sem.at[c]).wait()
        some = pl.ds(c * total, total - 1)
        pltpu.make_async_copy(recv.at[some], recv.at[some], r_sem.at[c]).wait()

    def left(c):
        some = pl.ds(c * total, total - 1)
        pltpu.make_async_copy(send.at[some], send.at[some], s_sem.at[c]).wait()

    def halo_copy(g):
        cols = pl.ds(g * L, L)
        back = lax.select(tm == 0, total - n_inp + inp, me - n_inp)
        return pltpu.make_async_remote_copy(
            volt.at[:, cols],
            halo.at[:, cols],
            hs_sem.at[g],
            hr_sem.at[g],
            device_id=back,
            device_id_type=LOGICAL,
        )

    def halo_ready(g):
        halo_copy(g).wait_recv()

        @pl.when(tm == n_time - 1)
        def _():
            halo[:, g * L : (g + 1) * L] = jnp.zeros((rows, L), jnp.bfloat16)

    gain_b[...] = jnp.broadcast_to(gain[...], (LANES, rows)).T
    feed_b[...] = jnp.broadcast_to(feed[...], (LANES, inputs)).T
    filter_frame(0)
    transform_frame(0)
    pl.semaphore_wait(barrier, total - 1)
    for g in range(TAPS - 1):
        halo_copy(g).start()

    def steer(i, carry):
        at = pl.ds(pl.multiple_of(i * step_rows, step_rows), step_rows)
        turns = jnp.concatenate([feed_b[at, :]] * (grid.shape[1] // LANES), 1) * grid[...]
        c, s = steer_block(turns, 1.0 / math.sqrt(inputs))
        cosine[at, :] = c
        sine[at, :] = s
        return carry

    lax.fori_loop(0, inputs // step_rows, steer, 0)
    for f in range(1, frames):
        halo_ready(f - 1)
        filter_frame(f)
        transform_frame(f)
        if f % PAIR == PAIR - 1:
            ship(f // PAIR)

    for c in range(chunks - 1):
        arrived(c)
        arrange(recv, c * total, n_time, n_inp, spec, turn, spec_t, turn_t)
        width = 256

        def products(j, carry):
            cols = pl.ds(pl.multiple_of(j * width, width), width)
            for ch in range(2):
                right = spec[ch, :, cols]
                sums[ch, 0, :, cols] = jnp.dot(spec_t[ch], right, preferred_element_type=jnp.float32)
                sums[ch, 1, :, cols] = jnp.dot(turn_t[ch], right, preferred_element_type=jnp.float32)
                power[ch, :, cols] = beam_sum(spec, turn, cosine, sine, ch, cols)
            return carry

        lax.fori_loop(0, inputs // width, products, 0)
    arrived(chunks - 1)
    for c in range(chunks):
        left(c)
    for g in range(TAPS - 1):
        halo_copy(g).wait_send()


def exchange(volt, gain, feed, grid, n_time, n_inp):
    rows = volt.shape[0]
    frames = volt.shape[1] // L
    chunks = frames // PAIR
    blocks = chunks * n_time * n_inp
    inputs = feed.shape[1]
    beams = grid.shape[1]
    depth = n_time * 4
    vmem = pl.BlockSpec(memory_space=pltpu.VMEM)
    dma = pltpu.SemaphoreType.DMA
    return pl.pallas_call(
        functools.partial(exchange_kernel, n_time, n_inp),
        name="exchange",
        out_shape=(
            jax.ShapeDtypeStruct((blocks, 8, rows), jnp.bfloat16),
            jax.ShapeDtypeStruct((inputs, beams), jnp.bfloat16),
            jax.ShapeDtypeStruct((inputs, beams), jnp.bfloat16),
            jax.ShapeDtypeStruct((2, 2, inputs, inputs), jnp.float32),
            jax.ShapeDtypeStruct((2, 1, beams), jnp.float32),
        ),
        in_specs=[vmem] * 6,
        out_specs=(vmem,) * 5,
        scratch_shapes=[
            pltpu.VMEM((rows, L), jnp.bfloat16),
            pltpu.VMEM((rows // LANES, 2 * CH * PAIR, LANES), jnp.float32),
            pltpu.VMEM((blocks, 8, rows), jnp.bfloat16),
            pltpu.VMEM((rows, (TAPS - 1) * L), jnp.bfloat16),
            pltpu.VMEM((rows, LANES), jnp.float32),
            pltpu.VMEM((inputs, LANES), jnp.int32),
            pltpu.VMEM((2, depth, inputs), jnp.bfloat16),
            pltpu.VMEM((2, depth, inputs), jnp.bfloat16),
            pltpu.VMEM((2, inputs, depth), jnp.bfloat16),
            pltpu.VMEM((2, inputs, depth), jnp.bfloat16),
            dma((chunks,)),
            dma((chunks,)),
            dma((TAPS - 1,)),
            dma((TAPS - 1,)),
            dma((chunks,)),
        ],
        compiler_params=pltpu.CompilerParams(collective_id=0, has_side_effects=True, vmem_limit_bytes=24 << 20),
    )(volt, gain, jnp.asarray(window_table()), jnp.asarray(dft_table()), feed, grid)


def products_kernel(n_time, n_inp, recv, cosine, sine, sums, part, visible, power, spec, turn, spec_t, turn_t):
    ch = pl.program_id(0)
    j = pl.program_id(1)

    @pl.when((ch == 0) & (j == 0))
    def _():
        arrange(recv, n_time * n_inp, n_time, n_inp, spec, turn, spec_t, turn_t)

    width = visible.shape[-1]
    cols = pl.ds(pl.multiple_of(j * width, width), width)
    right = spec[ch, :, cols]
    scale = 1.0 / (4 * n_time)
    for p, left in ((0, spec_t), (1, turn_t)):
        total = sums[ch, p, :, cols] + jnp.dot(left[ch], right, preferred_element_type=jnp.float32)
        visible[0, p] = (total * scale).astype(jnp.bfloat16)
    power[pl.ds(ch, 1), cols] = (part[ch, :, cols] + beam_sum(spec, turn, cosine, sine, ch, cols)) * scale


def products(recv, cosine, sine, sums, part, n_time, n_inp):
    inputs, beams = cosine.shape
    width = 256
    depth = n_time * 4
    vmem = pl.BlockSpec(memory_space=pltpu.VMEM)
    return pl.pallas_call(
        functools.partial(products_kernel, n_time, n_inp),
        name="products",
        grid=(2, inputs // width),
        out_shape=(
            jax.ShapeDtypeStruct((2, 2, inputs, inputs), jnp.bfloat16),
            jax.ShapeDtypeStruct((2, beams), jnp.float32),
        ),
        in_specs=[vmem] * 5,
        out_specs=(
            pl.BlockSpec((1, 2, inputs, width), lambda c, j: (c, 0, 0, j)),
            vmem,
        ),
        scratch_shapes=[
            pltpu.VMEM((2, depth, inputs), jnp.bfloat16),
            pltpu.VMEM((2, depth, inputs), jnp.bfloat16),
            pltpu.VMEM((2, inputs, depth), jnp.bfloat16),
            pltpu.VMEM((2, inputs, depth), jnp.bfloat16),
        ],
        compiler_params=pltpu.CompilerParams(vmem_limit_bytes=12 << 20),
    )(recv, cosine, sine, sums, part)


def on_device(voltages, input_gain, input_feed, beam_grid):
    n_time = lax.axis_size("tm")
    n_inp = lax.axis_size("inp")
    got = exchange(voltages, input_gain[None], input_feed[None], beam_grid[None], n_time, n_inp)
    return products(*got, n_time, n_inp)


def solution(mesh):
    return jax.shard_map(
        on_device,
        mesh=mesh,
        in_specs=(P("inp", "tm"), P("inp"), P(), P()),
        out_specs=(P(("tm", "inp"), None, None, None), P(("tm", "inp"), None)),
        check_vma=False,
    )
```

```python
import functools
import math

import jax
import jax.numpy as jnp
import numpy as np
from jax import lax
from jax.experimental import pallas as pl
from jax.experimental.pallas import tpu as pltpu
from jax.sharding import PartitionSpec as P

LOGICAL = pl.DeviceIdType.LOGICAL
L = 1024
CH = 512
TAPS = 4
GRID = 512
LANES = 128
PAIR = 2


def window_table():
    span = TAPS * L
    pos = np.arange(span).astype(np.float64)
    sinc_part = np.sinc((pos - span / 2) / L)
    hann_part = 0.5 - 0.5 * np.cos(2.0 * np.pi * pos / span)
    return (sinc_part * hann_part).reshape(TAPS, L).astype(np.float32)


def dft_table():
    step = np.arange(CH)[:, None] * np.arange(L)[None, :] % L
    radians = 2.0 * np.pi * step / L
    rows = np.stack([np.cos(radians), -np.sin(radians)], 1) / math.sqrt(L)
    return rows.reshape(2 * CH, L).astype(jnp.bfloat16)


def steer_block(phase, factor):
    phase = phase & (GRID - 1)
    turned = phase + GRID // 8
    quarter = (turned >> 7) & 3
    rest = (turned & 127) - GRID // 8
    x = rest.astype(jnp.float32) * (2.0 * math.pi / GRID)
    y = x * x
    sine = x * (1.0 + y * (-1.0 / 6 + y * (1.0 / 120 + y * (-1.0 / 5040 + y * (1.0 / 362880)))))
    cosine = 1.0 + y * (-0.5 + y * (1.0 / 24 + y * (-1.0 / 720 + y * (1.0 / 40320))))
    swap = (quarter & 1) == 1
    c_sign = jnp.where((quarter == 1) | (quarter == 2), -factor, factor)
    s_sign = jnp.where(quarter >= 2, factor, -factor)
    c = jnp.where(swap, sine, cosine) * c_sign
    s = jnp.where(swap, cosine, sine) * s_sign
    return c.astype(jnp.bfloat16), s.astype(jnp.bfloat16)


def arrange(recv, first, n_time, n_inp, spec, turn, spec_t, turn_t):
    width = recv.shape[2]
    half = n_time // 2
    rows = half * 8
    row = lax.broadcasted_iota(jnp.int32, (half, 8, width), 1)
    low = row < 4
    real = (row & 2) == 0
    for g in range(n_inp):
        lanes = slice(g * width, (g + 1) * width)
        got = recv[first + g * n_time : first + (g + 1) * n_time].astype(jnp.float32).reshape(half, 2, 8, width)
        even, odd = got[:, 0], got[:, 1]
        for ch in range(2):
            if ch == 0:
                y = jnp.where(low, even, pltpu.roll(odd, 4, 1))
            else:
                y = jnp.where(low, pltpu.roll(even, 4, 1), odd)
            z = jnp.where(real, pltpu.roll(y, 6, 1), -pltpu.roll(y, 2, 1))
            y = y.reshape(rows, width)
            z = z.reshape(rows, width)
            spec[ch, :, lanes] = y.astype(jnp.bfloat16)
            turn[ch, :, lanes] = z.astype(jnp.bfloat16)
            spec_t[ch, lanes, :] = y.T.astype(jnp.bfloat16)
            turn_t[ch, lanes, :] = z.T.astype(jnp.bfloat16)


def beam_sum(spec, turn, cosine, sine, ch, cols):
    beams = jnp.dot(spec[ch], cosine[:, cols], preferred_element_type=jnp.float32) + jnp.dot(
        turn[ch], sine[:, cols], preferred_element_type=jnp.float32
    )
    return jnp.sum(beams * beams, axis=0, keepdims=True)


def exchange_kernel(
    n_time,
    n_inp,
    volt_h,
    gain_h,
    window_h,
    table_h,
    feed_h,
    grid_h,
    recv,
    cosine,
    sine,
    sums,
    power,
    volt,
    gain,
    window,
    table,
    feed,
    grid,
    filt,
    wide,
    send,
    halo,
    gain_b,
    feed_b,
    spec,
    turn,
    spec_t,
    turn_t,
    s_sem,
    r_sem,
    hs_sem,
    hr_sem,
    l_sem,
    in_sem,
):
    total = n_time * n_inp
    rows = volt.shape[0]
    inputs = feed.shape[1]
    frames = volt.shape[1] // L
    chunks = frames // PAIR
    tm = lax.axis_index("tm")
    inp = lax.axis_index("inp")
    me = tm * n_inp + inp
    barrier = pltpu.get_barrier_semaphore()
    loads = [
        pltpu.make_async_copy(there, here, in_sem.at[i])
        for i, (there, here) in enumerate(
            ((volt_h, volt), (window_h, window), (gain_h, gain), (feed_h, feed), (grid_h, grid), (table_h, table))
        )
    ]
    for load in loads:
        load.start()

    def others(visit):
        def one(d, carry):
            visit(d)
            return carry

        lax.fori_loop(me + 1, total, one, 0)
        lax.fori_loop(0, me, one, 0)

    with jax.named_scope("greet"):
        others(lambda d: pl.semaphore_signal(barrier, inc=1, device_id=d, device_id_type=LOGICAL))

    step_rows = 16

    def filter_frame(f):
        def one(i, carry):
            at = pl.ds(pl.multiple_of(i * step_rows, step_rows), step_rows)
            summed = None
            for tap in range(TAPS):
                g = f + tap
                if g < frames:
                    piece = volt[at, g * L : (g + 1) * L].astype(jnp.float32)
                else:
                    piece = halo[at, (g - frames) * L : (g - frames + 1) * L].astype(jnp.float32)
                term = piece * window[tap : tap + 1, :]
                summed = term if summed is None else summed + term
            scale = jnp.concatenate([gain_b[at, :]] * (L // LANES), 1)
            filt[at, :] = (summed * scale).astype(jnp.bfloat16)
            return carry

        lax.fori_loop(0, rows // step_rows, one, 0)

    def transform_frame(f):
        c, place = f // PAIR, f % PAIR
        block = 256
        for b in range(2 * CH // block):
            part = lax.dot_general(
                table[b * block : (b + 1) * block, :],
                filt[...],
                (((1,), (1,)), ((), ())),
                preferred_element_type=jnp.float32,
            )
            start = b * block * PAIR
            for h in range(rows // LANES):
                wide[h, pl.ds(start + place, block, stride=PAIR), :] = part[:, h * LANES : (h + 1) * LANES]
            if place == PAIR - 1:
                n = block * PAIR // 8
                for h in range(rows // LANES):
                    ready = wide[h, start : start + block * PAIR, :].astype(jnp.bfloat16).reshape(n, 8, LANES)
                    send[c * total + b * n : c * total + (b + 1) * n, :, h * LANES : (h + 1) * LANES] = ready

    def ship(c):
        slot = c * total + inp * n_time + tm

        def one(d):
            pltpu.make_async_remote_copy(
                send.at[c * total + d],
                recv.at[slot],
                s_sem.at[c],
                r_sem.at[c],
                device_id=d,
                device_id_type=LOGICAL,
            ).start()

        others(one)
        pltpu.make_async_copy(send.at[c * total + me], recv.at[slot], l_sem.at[c]).start()

    def arrived(c):
        slot = c * total + inp * n_time + tm
        pltpu.make_async_copy(send.at[c * total + me], recv.at[slot], l_sem.at[c]).wait()
        some = pl.ds(c * total, total - 1)
        pltpu.make_async_copy(recv.at[some], recv.at[some], r_sem.at[c]).wait()

    def left(c):
        some = pl.ds(c * total, total - 1)
        pltpu.make_async_copy(send.at[some], send.at[some], s_sem.at[c]).wait()

    def halo_copy(g):
        cols = pl.ds(g * L, L)
        back = lax.select(tm == 0, total - n_inp + inp, me - n_inp)
        return pltpu.make_async_remote_copy(
            volt.at[:, cols],
            halo.at[:, cols],
            hs_sem.at[g],
            hr_sem.at[g],
            device_id=back,
            device_id_type=LOGICAL,
        )

    def halo_ready(g):
        halo_copy(g).wait_recv()

        @pl.when(tm == n_time - 1)
        def _():
            halo[:, g * L : (g + 1) * L] = jnp.zeros((rows, L), jnp.bfloat16)

    with jax.named_scope("load"):
        for load in loads:
            load.wait()
        gain_b[...] = jnp.broadcast_to(gain[...], (LANES, rows)).T
        feed_b[...] = jnp.broadcast_to(feed[...], (LANES, inputs)).T
    with jax.named_scope("filter0"):
        filter_frame(0)
    with jax.named_scope("transform0"):
        transform_frame(0)
    with jax.named_scope("barrier"):
        pl.semaphore_wait(barrier, total - 1)
    for g in range(TAPS - 1):
        halo_copy(g).start()

    def steer(i, carry):
        at = pl.ds(pl.multiple_of(i * step_rows, step_rows), step_rows)
        turns = jnp.concatenate([feed_b[at, :]] * (grid.shape[1] // LANES), 1) * grid[...]
        c, s = steer_block(turns, 1.0 / math.sqrt(inputs))
        cosine[at, :] = c
        sine[at, :] = s
        return carry

    with jax.named_scope("steer"):
        lax.fori_loop(0, inputs // step_rows, steer, 0)
    for f in range(1, frames):
        with jax.named_scope(f"halo{f}"):
            halo_ready(f - 1)
        with jax.named_scope(f"filter{f}"):
            filter_frame(f)
        with jax.named_scope(f"transform{f}"):
            transform_frame(f)
        if f % PAIR == PAIR - 1:
            with jax.named_scope(f"ship{f}"):
                ship(f // PAIR)

    for c in range(chunks - 1):
        with jax.named_scope("arrive"):
            arrived(c)
        with jax.named_scope("arrange"):
            arrange(recv, c * total, n_time, n_inp, spec, turn, spec_t, turn_t)
        width = 256

        def products(j, carry):
            cols = pl.ds(pl.multiple_of(j * width, width), width)
            for ch in range(2):
                right = spec[ch, :, cols]
                sums[ch, 0, :, cols] = jnp.dot(spec_t[ch], right, preferred_element_type=jnp.float32)
                sums[ch, 1, :, cols] = jnp.dot(turn_t[ch], right, preferred_element_type=jnp.float32)
                power[ch, :, cols] = beam_sum(spec, turn, cosine, sine, ch, cols)
            return carry

        with jax.named_scope("products"):
            lax.fori_loop(0, inputs // width, products, 0)
    with jax.named_scope("final"):
        arrived(chunks - 1)
    with jax.named_scope("left"):
        for c in range(chunks):
            left(c)
        for g in range(TAPS - 1):
            halo_copy(g).wait_send()


def exchange(volt, gain, feed, grid, n_time, n_inp):
    rows = volt.shape[0]
    frames = volt.shape[1] // L
    chunks = frames // PAIR
    blocks = chunks * n_time * n_inp
    inputs = feed.shape[1]
    beams = grid.shape[1]
    depth = n_time * 4
    vmem = pl.BlockSpec(memory_space=pltpu.VMEM)
    dma = pltpu.SemaphoreType.DMA
    return pl.pallas_call(
        functools.partial(exchange_kernel, n_time, n_inp),
        name="exchange",
        out_shape=(
            jax.ShapeDtypeStruct((blocks, 8, rows), jnp.bfloat16),
            jax.ShapeDtypeStruct((inputs, beams), jnp.bfloat16),
            jax.ShapeDtypeStruct((inputs, beams), jnp.bfloat16),
            jax.ShapeDtypeStruct((2, 2, inputs, inputs), jnp.float32),
            jax.ShapeDtypeStruct((2, 1, beams), jnp.float32),
        ),
        in_specs=[pl.BlockSpec(memory_space=pltpu.HBM)] * 6,
        out_specs=(vmem,) * 5,
        scratch_shapes=[
            pltpu.VMEM(volt.shape, volt.dtype),
            pltpu.VMEM(gain.shape, gain.dtype),
            pltpu.VMEM((TAPS, L), jnp.float32),
            pltpu.VMEM((2 * CH, L), jnp.bfloat16),
            pltpu.VMEM(feed.shape, feed.dtype),
            pltpu.VMEM(grid.shape, grid.dtype),
            pltpu.VMEM((rows, L), jnp.bfloat16),
            pltpu.VMEM((rows // LANES, 2 * CH * PAIR, LANES), jnp.float32),
            pltpu.VMEM((blocks, 8, rows), jnp.bfloat16),
            pltpu.VMEM((rows, (TAPS - 1) * L), jnp.bfloat16),
            pltpu.VMEM((rows, LANES), jnp.float32),
            pltpu.VMEM((inputs, LANES), jnp.int32),
            pltpu.VMEM((2, depth, inputs), jnp.bfloat16),
            pltpu.VMEM((2, depth, inputs), jnp.bfloat16),
            pltpu.VMEM((2, inputs, depth), jnp.bfloat16),
            pltpu.VMEM((2, inputs, depth), jnp.bfloat16),
            dma((chunks,)),
            dma((chunks,)),
            dma((TAPS - 1,)),
            dma((TAPS - 1,)),
            dma((chunks,)),
            dma((6,)),
        ],
        compiler_params=pltpu.CompilerParams(collective_id=0, has_side_effects=True, vmem_limit_bytes=24 << 20),
    )(*(pltpu.with_memory_space_constraint(a, pltpu.HBM) for a in (volt, gain, jnp.asarray(window_table()), jnp.asarray(dft_table()), feed, grid)))


def products_kernel(n_time, n_inp, recv, cosine, sine, sums, part, visible, power, spec, turn, spec_t, turn_t):
    ch = pl.program_id(0)
    j = pl.program_id(1)

    @pl.when((ch == 0) & (j == 0))
    def _():
        arrange(recv, n_time * n_inp, n_time, n_inp, spec, turn, spec_t, turn_t)

    width = visible.shape[-1]
    cols = pl.ds(pl.multiple_of(j * width, width), width)
    right = spec[ch, :, cols]
    scale = 1.0 / (4 * n_time)
    for p, left in ((0, spec_t), (1, turn_t)):
        total = sums[ch, p, :, cols] + jnp.dot(left[ch], right, preferred_element_type=jnp.float32)
        visible[0, p] = (total * scale).astype(jnp.bfloat16)
    power[pl.ds(ch, 1), cols] = (part[ch, :, cols] + beam_sum(spec, turn, cosine, sine, ch, cols)) * scale


def products(recv, cosine, sine, sums, part, n_time, n_inp):
    inputs, beams = cosine.shape
    width = 256
    depth = n_time * 4
    vmem = pl.BlockSpec(memory_space=pltpu.VMEM)
    return pl.pallas_call(
        functools.partial(products_kernel, n_time, n_inp),
        name="products",
        grid=(2, inputs // width),
        out_shape=(
            jax.ShapeDtypeStruct((2, 2, inputs, inputs), jnp.bfloat16),
            jax.ShapeDtypeStruct((2, beams), jnp.float32),
        ),
        in_specs=[vmem] * 5,
        out_specs=(
            pl.BlockSpec((1, 2, inputs, width), lambda c, j: (c, 0, 0, j)),
            vmem,
        ),
        scratch_shapes=[
            pltpu.VMEM((2, depth, inputs), jnp.bfloat16),
            pltpu.VMEM((2, depth, inputs), jnp.bfloat16),
            pltpu.VMEM((2, inputs, depth), jnp.bfloat16),
            pltpu.VMEM((2, inputs, depth), jnp.bfloat16),
        ],
        compiler_params=pltpu.CompilerParams(vmem_limit_bytes=12 << 20),
    )(recv, cosine, sine, sums, part)


def on_device(voltages, input_gain, input_feed, beam_grid):
    n_time = lax.axis_size("tm")
    n_inp = lax.axis_size("inp")
    got = exchange(voltages, input_gain[None], input_feed[None], beam_grid[None], n_time, n_inp)
    return products(*got, n_time, n_inp)


def solution(mesh):
    return jax.shard_map(
        on_device,
        mesh=mesh,
        in_specs=(P("inp", "tm"), P("inp"), P(), P()),
        out_specs=(P(("tm", "inp"), None, None, None), P(("tm", "inp"), None)),
        check_vma=False,
    )
```

```python
import functools
import math

import jax
import jax.numpy as jnp
import numpy as np
from jax import lax
from jax.experimental import pallas as pl
from jax.experimental.pallas import tpu as pltpu
from jax.sharding import PartitionSpec as P

LOGICAL = pl.DeviceIdType.LOGICAL
L = 1024
CH = 512
TAPS = 4
GRID = 512
LANES = 128
PAIR = 2


def window_table():
    span = TAPS * L
    pos = np.arange(span).astype(np.float64)
    sinc_part = np.sinc((pos - span / 2) / L)
    hann_part = 0.5 - 0.5 * np.cos(2.0 * np.pi * pos / span)
    return (sinc_part * hann_part).reshape(TAPS, L).astype(np.float32)


def dft_table(n_time, n_inp):
    step = np.arange(CH)[:, None] * np.arange(L)[None, :] % L
    radians = 2.0 * np.pi * step / L
    rows = np.stack([np.cos(radians), -np.sin(radians)], 1) / math.sqrt(L)
    rows = rows.reshape(n_time // 4, 2, 2, n_inp, -1, L).transpose(3, 1, 0, 2, 4, 5)
    return rows.reshape(2 * CH, L).astype(jnp.bfloat16)


def steer_block(phase, factor):
    phase = phase & (GRID - 1)
    turned = phase + GRID // 8
    quarter = (turned >> 7) & 3
    rest = (turned & 127) - GRID // 8
    x = rest.astype(jnp.float32) * (2.0 * math.pi / GRID)
    y = x * x
    sine = x * (1.0 + y * (-1.0 / 6 + y * (1.0 / 120 + y * (-1.0 / 5040 + y * (1.0 / 362880)))))
    cosine = 1.0 + y * (-0.5 + y * (1.0 / 24 + y * (-1.0 / 720 + y * (1.0 / 40320))))
    swap = (quarter & 1) == 1
    c_sign = jnp.where((quarter == 1) | (quarter == 2), -factor, factor)
    s_sign = jnp.where(quarter >= 2, factor, -factor)
    c = jnp.where(swap, sine, cosine) * c_sign
    s = jnp.where(swap, cosine, sine) * s_sign
    return c.astype(jnp.bfloat16), s.astype(jnp.bfloat16)


def arrange(recv, first, n_time, n_inp, spec, turn, spec_t, turn_t):
    width = recv.shape[2]
    half = n_time // 2
    rows = half * 8
    row = lax.broadcasted_iota(jnp.int32, (half, 8, width), 1)
    low = row < 4
    real = (row & 2) == 0
    for g in range(n_inp):
        lanes = slice(g * width, (g + 1) * width)
        got = recv[first + g * n_time : first + (g + 1) * n_time].astype(jnp.float32).reshape(half, 2, 8, width)
        even, odd = got[:, 0], got[:, 1]
        for ch in range(2):
            if ch == 0:
                y = jnp.where(low, even, pltpu.roll(odd, 4, 1))
            else:
                y = jnp.where(low, pltpu.roll(even, 4, 1), odd)
            z = jnp.where(real, pltpu.roll(y, 6, 1), -pltpu.roll(y, 2, 1))
            y = y.reshape(rows, width)
            z = z.reshape(rows, width)
            spec[ch, :, lanes] = y.astype(jnp.bfloat16)
            turn[ch, :, lanes] = z.astype(jnp.bfloat16)
            spec_t[ch, lanes, :] = y.T.astype(jnp.bfloat16)
            turn_t[ch, lanes, :] = z.T.astype(jnp.bfloat16)


def beam_sum(spec, turn, cosine, sine, ch, cols):
    beams = jnp.dot(spec[ch], cosine[:, cols], preferred_element_type=jnp.float32) + jnp.dot(
        turn[ch], sine[:, cols], preferred_element_type=jnp.float32
    )
    return jnp.sum(beams * beams, axis=0, keepdims=True)


def exchange_kernel(
    n_time,
    n_inp,
    volt_h,
    gain_h,
    window_h,
    table_h,
    feed_h,
    grid_h,
    recv,
    cosine,
    sine,
    sums,
    power,
    volt,
    gain,
    window,
    table,
    feed,
    grid,
    filt,
    wide,
    send,
    send_b,
    halo,
    split,
    outward,
    inward,
    gain_b,
    feed_b,
    spec,
    turn,
    spec_t,
    turn_t,
    s_sem,
    b_sem,
    r_sem,
    hs_sem,
    hr_sem,
    xs_sem,
    xr_sem,
    in_sem,
):
    total = n_time * n_inp
    rows = volt.shape[0]
    inputs = feed.shape[1]
    frames = volt.shape[1] // L
    chunks = frames // PAIR
    n_yx, n_z = n_time // 4, 2 * n_inp
    sides = n_z // 2
    group = 2 * CH // n_z
    owners = group // 4
    tm = lax.axis_index("tm")
    inp = lax.axis_index("inp")
    me = tm * n_inp + inp
    core = lax.rem(tm, 2)
    z_lo = lax.rem(tm // 2, 2)
    yx = tm // 4
    z = 2 * inp + z_lo
    way = 2 * z_lo - 1
    kept = [lax.rem(z + way * t + n_z, n_z) for t in range(sides)]
    given = [lax.rem(z - way * (t + 1) + n_z, n_z) for t in range(sides)]
    partner_tm = lax.rem(tm + 2 * core - 1 + n_time, n_time)
    source_tm = lax.rem(tm + core - 1 + n_time, n_time)
    barrier = pltpu.get_barrier_semaphore()
    loads = [
        pltpu.make_async_copy(there, here, in_sem.at[i])
        for i, (there, here) in enumerate(
            ((volt_h, volt), (window_h, window), (gain_h, gain), (feed_h, feed), (grid_h, grid), (table_h, table))
        )
    ]
    for load in loads:
        load.start()

    def greet(d, carry):
        pl.semaphore_signal(barrier, inc=1, device_id=d, device_id_type=LOGICAL)
        return carry

    with jax.named_scope("greet"):
        lax.fori_loop(me + 1, total, greet, 0)
        lax.fori_loop(0, me, greet, 0)

    step_rows = 16

    def filter_frame(f, kind):
        def one(i, carry):
            at = pl.ds(pl.multiple_of(i * step_rows, step_rows), step_rows)
            summed = None
            for tap in range(TAPS):
                g = f + tap
                if (kind == "near" and g >= frames) or (kind == "far" and g < frames):
                    continue
                if kind == "full" and g >= frames:
                    piece = halo[at, (g - frames) * L : (g - frames + 1) * L]
                else:
                    piece = volt[at, g % frames * L : (g % frames + 1) * L]
                term = piece.astype(jnp.float32) * window[tap : tap + 1, :]
                summed = term if summed is None else summed + term
            scale = gain_b[at, :]
            if kind == "far":
                scale = jnp.where(tm == 0, 0.0, scale)
            scale = jnp.concatenate([scale] * (L // LANES), 1)
            filt[at, :] = (summed * scale).astype(jnp.bfloat16)
            return carry

        lax.fori_loop(0, rows // step_rows, one, 0)

    block = 256

    def spectrum(b):
        return lax.dot_general(
            table[pl.ds(b * block, block), :], filt[...], (((1,), (1,)), ((), ())), preferred_element_type=jnp.float32
        )

    def pack(part, place, first, count, target, at):
        for h in range(rows // LANES):
            wide[h, pl.ds(first * PAIR + place, count, stride=PAIR), :] = part[:, h * LANES : (h + 1) * LANES]
        if place == PAIR - 1:
            n = count * PAIR // 8
            for h in range(rows // LANES):
                ready = wide[h, first * PAIR : (first + count) * PAIR, :].astype(jnp.bfloat16).reshape(n, 8, LANES)
                target[at : at + n, :, h * LANES : (h + 1) * LANES] = ready

    def transform_whole(f):
        for b in range(2 * CH // block):
            pack(spectrum(b), f % PAIR, b * block, block, send, f // PAIR * total + b * block // 4)

    def transform_part(f):
        for b in range(2 * CH // block):
            split[f, b * block : (b + 1) * block, :] = spectrum(b)
        for t in range(sides):
            at = pl.ds(pl.multiple_of(given[t] * group, group), group)
            outward[f, t] = split[f, at, :].astype(jnp.bfloat16)

    def combine(f):
        for t in range(sides):
            at = pl.ds(pl.multiple_of(kept[t] * group, group), group)
            part = split[f, at, :] + inward[f, t].astype(jnp.float32)
            pack(part, f % PAIR, t * group, group, send_b, f // PAIR * sides * owners + t * owners)

    def ship(source, starts, levels, source_tm, c, sem):
        slot = c * total + inp * n_time + source_tm
        firsts = [lax.rem(v, 2) * 2 * n_inp + v // 2 for v in levels]

        def copy(row, i, side):
            pltpu.make_async_remote_copy(
                source.at[starts[i] + row * 2 + side],
                recv.at[slot],
                sem.at[c],
                r_sem.at[c],
                device_id=row * 4 * n_inp + firsts[i] + side * n_inp,
                device_id_type=LOGICAL,
            ).start()

        def one(row, carry):
            for i in range(len(levels)):
                for side in range(2):
                    copy(row, i, side)
            return carry

        lax.fori_loop(yx + 1, n_yx, one, 0)
        copy(yx, 0, 1 - core)
        for i in range(1, len(levels)):
            for side in range(2):
                copy(yx, i, side)
        lax.fori_loop(0, yx, one, 0)
        pltpu.make_async_copy(source.at[starts[0] + yx * 2 + core], recv.at[slot], r_sem.at[c]).start()

    def arrived(c):
        some = pl.ds(c * total, total)
        pltpu.make_async_copy(recv.at[some], recv.at[some], r_sem.at[c]).wait()

    def halo_copy(g):
        cols = pl.ds(g * L, L)
        return pltpu.make_async_remote_copy(
            volt.at[:, cols],
            halo.at[:, cols],
            hs_sem.at[g],
            hr_sem.at[g],
            device_id=me - n_inp,
            device_id_type=LOGICAL,
        )

    def part_copy(f):
        return pltpu.make_async_remote_copy(
            outward.at[f],
            inward.at[f],
            xs_sem.at[f],
            xr_sem.at[f],
            device_id=partner_tm * n_inp + inp,
            device_id_type=LOGICAL,
        )

    with jax.named_scope("load"):
        for load in loads:
            load.wait()
        gain_b[...] = jnp.broadcast_to(gain[...], (LANES, rows)).T
        feed_b[...] = jnp.broadcast_to(feed[...], (LANES, inputs)).T

    @pl.when(core == 1)
    def _():
        with jax.named_scope("near"):
            inward[0] = jnp.zeros(inward.shape[1:], inward.dtype)
            for f in range(frames):
                filter_frame(f, "near")
                transform_part(f)

    @pl.when(core == 0)
    def _():
        with jax.named_scope("far"):
            split[0] = jnp.zeros(split.shape[1:], split.dtype)
            for f in range(1, frames):
                filter_frame(f, "far")
                transform_part(f)

    with jax.named_scope("barrier"):
        pl.semaphore_wait(barrier, total - 1)

    @pl.when(core == 1)
    def _():
        for g in range(TAPS - 1):
            halo_copy(g).start()
        for f in range(frames):
            part_copy(f).start()

    @pl.when(core == 0)
    def _():
        for f in range(1, frames):
            part_copy(f).start()
        levels = [lax.rem(z + u, n_z) for u in range(n_z)]
        for f in range(frames):
            if f:
                with jax.named_scope(f"halo{f}"):
                    halo_copy(f - 1).wait_recv()
            with jax.named_scope(f"whole{f}"):
                filter_frame(f, "full")
                transform_whole(f)
            if f % PAIR == PAIR - 1:
                c = f // PAIR
                with jax.named_scope(f"ship{f}"):
                    ship(send, [c * total + v * owners for v in levels], levels, tm, c, s_sem)

    def steer(i, carry):
        at = pl.ds(pl.multiple_of(i * step_rows, step_rows), step_rows)
        turns = jnp.concatenate([feed_b[at, :]] * (grid.shape[1] // LANES), 1) * grid[...]
        c, s = steer_block(turns, 1.0 / math.sqrt(inputs))
        cosine[at, :] = c
        sine[at, :] = s
        return carry

    with jax.named_scope("steer"):
        lax.fori_loop(0, inputs // step_rows, steer, 0)

    for f in range(frames):
        with jax.named_scope(f"part{f}"):
            if f:
                part_copy(f).wait_recv()
            else:

                @pl.when(core == 0)
                def _():
                    part_copy(0).wait_recv()

        with jax.named_scope(f"combine{f}"):
            combine(f)
        if f % PAIR == PAIR - 1:
            c = f // PAIR
            with jax.named_scope(f"shipb{f}"):
                starts = [(c * sides + t) * owners for t in range(sides)]
                ship(send_b, starts, kept, source_tm, c, b_sem)

    for c in range(chunks - 1):
        with jax.named_scope("arrive"):
            arrived(c)
        with jax.named_scope("arrange"):
            arrange(recv, c * total, n_time, n_inp, spec, turn, spec_t, turn_t)
        width = 256

        def products(j, carry):
            cols = pl.ds(pl.multiple_of(j * width, width), width)
            for ch in range(2):
                right = spec[ch, :, cols]
                sums[ch, 0, :, cols] = jnp.dot(spec_t[ch], right, preferred_element_type=jnp.float32)
                sums[ch, 1, :, cols] = jnp.dot(turn_t[ch], right, preferred_element_type=jnp.float32)
                power[ch, :, cols] = beam_sum(spec, turn, cosine, sine, ch, cols)
            return carry

        with jax.named_scope("products"):
            lax.fori_loop(0, inputs // width, products, 0)
    with jax.named_scope("final"):
        arrived(chunks - 1)

    with jax.named_scope("left"):
        for c in range(chunks):
            some = pl.ds(0, sides * owners - 1)
            pltpu.make_async_copy(send_b.at[some], send_b.at[some], b_sem.at[c]).wait()
        for f in range(1, frames):
            part_copy(f).wait_send()

        @pl.when(core == 1)
        def _():
            part_copy(0).wait_send()
            for g in range(TAPS - 1):
                halo_copy(g).wait_send()

        @pl.when(core == 0)
        def _():
            for c in range(chunks):
                some = pl.ds(0, total - 1)
                pltpu.make_async_copy(send.at[some], send.at[some], s_sem.at[c]).wait()


def exchange(volt, gain, feed, grid, n_time, n_inp):
    rows = volt.shape[0]
    frames = volt.shape[1] // L
    chunks = frames // PAIR
    blocks = chunks * n_time * n_inp
    inputs = feed.shape[1]
    beams = grid.shape[1]
    depth = n_time * 4
    vmem = pl.BlockSpec(memory_space=pltpu.VMEM)
    dma = pltpu.SemaphoreType.DMA
    return pl.pallas_call(
        functools.partial(exchange_kernel, n_time, n_inp),
        name="exchange",
        out_shape=(
            jax.ShapeDtypeStruct((blocks, 8, rows), jnp.bfloat16),
            jax.ShapeDtypeStruct((inputs, beams), jnp.bfloat16),
            jax.ShapeDtypeStruct((inputs, beams), jnp.bfloat16),
            jax.ShapeDtypeStruct((2, 2, inputs, inputs), jnp.float32),
            jax.ShapeDtypeStruct((2, 1, beams), jnp.float32),
        ),
        in_specs=[pl.BlockSpec(memory_space=pltpu.HBM)] * 6,
        out_specs=(vmem,) * 5,
        scratch_shapes=[
            pltpu.VMEM(volt.shape, volt.dtype),
            pltpu.VMEM(gain.shape, gain.dtype),
            pltpu.VMEM((TAPS, L), jnp.float32),
            pltpu.VMEM((2 * CH, L), jnp.bfloat16),
            pltpu.VMEM(feed.shape, feed.dtype),
            pltpu.VMEM(grid.shape, grid.dtype),
            pltpu.VMEM((rows, L), jnp.bfloat16),
            pltpu.VMEM((rows // LANES, 2 * CH * PAIR, LANES), jnp.float32),
            pltpu.VMEM((blocks, 8, rows), jnp.bfloat16),
            pltpu.VMEM((blocks // 2, 8, rows), jnp.bfloat16),
            pltpu.VMEM((rows, (TAPS - 1) * L), jnp.bfloat16),
            pltpu.VMEM((frames, 2 * CH, rows), jnp.float32),
            pltpu.VMEM((frames, n_inp, CH // n_inp, rows), jnp.bfloat16),
            pltpu.VMEM((frames, n_inp, CH // n_inp, rows), jnp.bfloat16),
            pltpu.VMEM((rows, LANES), jnp.float32),
            pltpu.VMEM((inputs, LANES), jnp.int32),
            pltpu.VMEM((2, depth, inputs), jnp.bfloat16),
            pltpu.VMEM((2, depth, inputs), jnp.bfloat16),
            pltpu.VMEM((2, inputs, depth), jnp.bfloat16),
            pltpu.VMEM((2, inputs, depth), jnp.bfloat16),
            dma((chunks,)),
            dma((chunks,)),
            dma((chunks,)),
            dma((TAPS - 1,)),
            dma((TAPS - 1,)),
            dma((frames,)),
            dma((frames,)),
            dma((6,)),
        ],
        compiler_params=pltpu.CompilerParams(collective_id=0, has_side_effects=True, vmem_limit_bytes=30 << 20),
    )(*(pltpu.with_memory_space_constraint(a, pltpu.HBM) for a in (volt, gain, jnp.asarray(window_table()), jnp.asarray(dft_table(n_time, n_inp)), feed, grid)))


def products_kernel(n_time, n_inp, recv, cosine, sine, sums, part, visible, power, spec, turn, spec_t, turn_t):
    ch = pl.program_id(0)
    j = pl.program_id(1)

    @pl.when((ch == 0) & (j == 0))
    def _():
        arrange(recv, n_time * n_inp, n_time, n_inp, spec, turn, spec_t, turn_t)

    width = visible.shape[-1]
    cols = pl.ds(pl.multiple_of(j * width, width), width)
    right = spec[ch, :, cols]
    scale = 1.0 / (4 * n_time)
    for p, left in ((0, spec_t), (1, turn_t)):
        total = sums[ch, p, :, cols] + jnp.dot(left[ch], right, preferred_element_type=jnp.float32)
        visible[0, p] = (total * scale).astype(jnp.bfloat16)
    power[pl.ds(ch, 1), cols] = (part[ch, :, cols] + beam_sum(spec, turn, cosine, sine, ch, cols)) * scale


def products(recv, cosine, sine, sums, part, n_time, n_inp):
    inputs, beams = cosine.shape
    width = 256
    depth = n_time * 4
    vmem = pl.BlockSpec(memory_space=pltpu.VMEM)
    return pl.pallas_call(
        functools.partial(products_kernel, n_time, n_inp),
        name="products",
        grid=(2, inputs // width),
        out_shape=(
            jax.ShapeDtypeStruct((2, 2, inputs, inputs), jnp.bfloat16),
            jax.ShapeDtypeStruct((2, beams), jnp.float32),
        ),
        in_specs=[vmem] * 5,
        out_specs=(
            pl.BlockSpec((1, 2, inputs, width), lambda c, j: (c, 0, 0, j)),
            vmem,
        ),
        scratch_shapes=[
            pltpu.VMEM((2, depth, inputs), jnp.bfloat16),
            pltpu.VMEM((2, depth, inputs), jnp.bfloat16),
            pltpu.VMEM((2, inputs, depth), jnp.bfloat16),
            pltpu.VMEM((2, inputs, depth), jnp.bfloat16),
        ],
        compiler_params=pltpu.CompilerParams(vmem_limit_bytes=12 << 20),
    )(recv, cosine, sine, sums, part)


def on_device(voltages, input_gain, input_feed, beam_grid):
    n_time = lax.axis_size("tm")
    n_inp = lax.axis_size("inp")
    got = exchange(voltages, input_gain[None], input_feed[None], beam_grid[None], n_time, n_inp)
    return products(*got, n_time, n_inp)


def solution(mesh):
    return jax.shard_map(
        on_device,
        mesh=mesh,
        in_specs=(P("inp", "tm"), P("inp"), P(), P()),
        out_specs=(P(("tm", "inp"), None, None, None), P(("tm", "inp"), None)),
        check_vma=False,
    )
```

```python
import functools
import math

import jax
import jax.numpy as jnp
import numpy as np
from jax import lax
from jax.experimental import pallas as pl
from jax.experimental.pallas import tpu as pltpu
from jax.sharding import PartitionSpec as P

LOGICAL = pl.DeviceIdType.LOGICAL
L = 1024
CH = 512
TAPS = 4
GRID = 512
LANES = 128
PAIR = 2


def window_table():
    span = TAPS * L
    pos = np.arange(span).astype(np.float64)
    sinc_part = np.sinc((pos - span / 2) / L)
    hann_part = 0.5 - 0.5 * np.cos(2.0 * np.pi * pos / span)
    return (sinc_part * hann_part).reshape(TAPS, L).astype(np.float32)


def dft_table(n_time, n_inp):
    step = np.arange(CH)[:, None] * np.arange(L)[None, :] % L
    radians = 2.0 * np.pi * step / L
    rows = np.stack([np.cos(radians), -np.sin(radians)], 1) / math.sqrt(L)
    rows = rows.reshape(n_time // 4, 2, 2, n_inp, -1, L).transpose(3, 1, 0, 2, 4, 5)
    return rows.reshape(2 * CH, L).astype(jnp.bfloat16)


def steer_block(phase, factor):
    phase = phase & (GRID - 1)
    turned = phase + GRID // 8
    quarter = (turned >> 7) & 3
    rest = (turned & 127) - GRID // 8
    x = rest.astype(jnp.float32) * (2.0 * math.pi / GRID)
    y = x * x
    sine = x * (1.0 + y * (-1.0 / 6 + y * (1.0 / 120 + y * (-1.0 / 5040 + y * (1.0 / 362880)))))
    cosine = 1.0 + y * (-0.5 + y * (1.0 / 24 + y * (-1.0 / 720 + y * (1.0 / 40320))))
    swap = (quarter & 1) == 1
    c_sign = jnp.where((quarter == 1) | (quarter == 2), -factor, factor)
    s_sign = jnp.where(quarter >= 2, factor, -factor)
    c = jnp.where(swap, sine, cosine) * c_sign
    s = jnp.where(swap, cosine, sine) * s_sign
    return c.astype(jnp.bfloat16), s.astype(jnp.bfloat16)


def arrange(recv, first, n_time, n_inp, spec, turn, spec_t, turn_t):
    width = recv.shape[2]
    half = n_time // 2
    rows = half * 8
    row = lax.broadcasted_iota(jnp.int32, (half, 8, width), 1)
    low = row < 4
    real = (row & 2) == 0
    for g in range(n_inp):
        lanes = slice(g * width, (g + 1) * width)
        got = recv[first + g * n_time : first + (g + 1) * n_time].astype(jnp.float32).reshape(half, 2, 8, width)
        even, odd = got[:, 0], got[:, 1]
        for ch in range(2):
            if ch == 0:
                y = jnp.where(low, even, pltpu.roll(odd, 4, 1))
            else:
                y = jnp.where(low, pltpu.roll(even, 4, 1), odd)
            z = jnp.where(real, pltpu.roll(y, 6, 1), -pltpu.roll(y, 2, 1))
            y = y.reshape(rows, width)
            z = z.reshape(rows, width)
            spec[ch, :, lanes] = y.astype(jnp.bfloat16)
            turn[ch, :, lanes] = z.astype(jnp.bfloat16)
            spec_t[ch, lanes, :] = y.T.astype(jnp.bfloat16)
            turn_t[ch, lanes, :] = z.T.astype(jnp.bfloat16)


def beam_sum(spec, turn, cosine, sine, ch, cols):
    beams = jnp.dot(spec[ch], cosine[:, cols], preferred_element_type=jnp.float32) + jnp.dot(
        turn[ch], sine[:, cols], preferred_element_type=jnp.float32
    )
    return jnp.sum(beams * beams, axis=0, keepdims=True)


def exchange_kernel(
    n_time,
    n_inp,
    volt_h,
    gain_h,
    window_h,
    table_h,
    feed_h,
    grid_h,
    recv,
    cosine,
    sine,
    sums,
    power,
    volt,
    gain,
    window,
    table,
    feed,
    grid,
    filt,
    wide,
    send,
    send_b,
    halo,
    split,
    outward,
    inward,
    gain_b,
    feed_b,
    spec,
    turn,
    spec_t,
    turn_t,
    s_sem,
    b_sem,
    r_sem,
    hs_sem,
    hr_sem,
    xs_sem,
    xr_sem,
    in_sem,
):
    total = n_time * n_inp
    rows = volt.shape[0]
    inputs = feed.shape[1]
    frames = volt.shape[1] // L
    chunks = frames // PAIR
    n_yx, n_z = n_time // 4, 2 * n_inp
    sides = n_z // 2
    group = 2 * CH // n_z
    owners = group // 4
    tm = lax.axis_index("tm")
    inp = lax.axis_index("inp")
    me = tm * n_inp + inp
    core = lax.rem(tm, 2)
    z_lo = lax.rem(tm // 2, 2)
    yx = tm // 4
    z = 2 * inp + z_lo
    way = 2 * z_lo - 1
    kept = [lax.rem(z + way * t + n_z, n_z) for t in range(sides)]
    given = [lax.rem(z - way * (t + 1) + n_z, n_z) for t in range(sides)]
    partner_tm = lax.rem(tm + 2 * core - 1 + n_time, n_time)
    source_tm = lax.rem(tm + core - 1 + n_time, n_time)
    barrier = pltpu.get_barrier_semaphore()
    loads = [
        pltpu.make_async_copy(there, here, in_sem.at[i])
        for i, (there, here) in enumerate(
            ((volt_h, volt), (window_h, window), (gain_h, gain), (feed_h, feed), (grid_h, grid), (table_h, table))
        )
    ]
    for load in loads:
        load.start()

    def greet(d, carry):
        pl.semaphore_signal(barrier, inc=1, device_id=d, device_id_type=LOGICAL)
        return carry

    with jax.named_scope("greet"):
        lax.fori_loop(me + 1, total, greet, 0)
        lax.fori_loop(0, me, greet, 0)

    step_rows = 16

    def filter_frame(f, kind):
        def one(i, carry):
            at = pl.ds(pl.multiple_of(i * step_rows, step_rows), step_rows)
            summed = None
            for tap in range(TAPS):
                g = f + tap
                if (kind == "near" and g >= frames) or (kind == "far" and g < frames):
                    continue
                if kind == "full" and g >= frames:
                    piece = halo[at, (g - frames) * L : (g - frames + 1) * L]
                else:
                    piece = volt[at, g % frames * L : (g % frames + 1) * L]
                term = piece.astype(jnp.float32) * window[tap : tap + 1, :]
                summed = term if summed is None else summed + term
            scale = gain_b[at, :]
            if kind == "far":
                scale = jnp.where(tm == 0, 0.0, scale)
            scale = jnp.concatenate([scale] * (L // LANES), 1)
            filt[at, :] = (summed * scale).astype(jnp.bfloat16)
            return carry

        lax.fori_loop(0, rows // step_rows, one, 0)

    block = 256

    def spectrum(b):
        return lax.dot_general(
            table[pl.ds(b * block, block), :], filt[...], (((1,), (1,)), ((), ())), preferred_element_type=jnp.float32
        )

    def pack(part, place, first, count, target, at):
        for h in range(rows // LANES):
            wide[h, pl.ds(first * PAIR + place, count, stride=PAIR), :] = part[:, h * LANES : (h + 1) * LANES]
        if place == PAIR - 1:
            n = count * PAIR // 8
            for h in range(rows // LANES):
                ready = wide[h, first * PAIR : (first + count) * PAIR, :].astype(jnp.bfloat16).reshape(n, 8, LANES)
                target[at : at + n, :, h * LANES : (h + 1) * LANES] = ready

    def transform_whole(f):
        for b in range(2 * CH // block):
            pack(spectrum(b), f % PAIR, b * block, block, send, f // PAIR * total + b * block // 4)

    def transform_part(f):
        for b in range(2 * CH // block):
            split[f, b * block : (b + 1) * block, :] = spectrum(b)
        for t in range(sides):
            at = pl.ds(pl.multiple_of(given[t] * group, group), group)
            outward[f, t] = split[f, at, :].astype(jnp.bfloat16)

    def combine(f):
        for t in range(sides):
            at = pl.ds(pl.multiple_of(kept[t] * group, group), group)
            part = split[f, at, :] + inward[f, t].astype(jnp.float32)
            pack(part, f % PAIR, t * group, group, send_b, f // PAIR * sides * owners + t * owners)

    def ship(source, starts, levels, source_tm, c, sem):
        slot = c * total + inp * n_time + source_tm
        firsts = [lax.rem(v, 2) * 2 * n_inp + v // 2 for v in levels]

        def copy(row, i, side):
            pltpu.make_async_remote_copy(
                source.at[starts[i] + row * 2 + side],
                recv.at[slot],
                sem.at[c],
                r_sem.at[c],
                device_id=row * 4 * n_inp + firsts[i] + side * n_inp,
                device_id_type=LOGICAL,
            ).start()

        def one(row, carry):
            for i in range(len(levels)):
                for side in range(2):
                    copy(row, i, side)
            return carry

        lax.fori_loop(yx + 1, n_yx, one, 0)
        copy(yx, 0, 1 - core)
        for i in range(1, len(levels)):
            for side in range(2):
                copy(yx, i, side)
        lax.fori_loop(0, yx, one, 0)
        pltpu.make_async_copy(source.at[starts[0] + yx * 2 + core], recv.at[slot], r_sem.at[c]).start()

    def arrived(c):
        some = pl.ds(c * total, total)
        pltpu.make_async_copy(recv.at[some], recv.at[some], r_sem.at[c]).wait()

    def halo_copy(g):
        cols = pl.ds(g * L, L)
        return pltpu.make_async_remote_copy(
            volt.at[:, cols],
            halo.at[:, cols],
            hs_sem.at[g],
            hr_sem.at[g],
            device_id=me - n_inp,
            device_id_type=LOGICAL,
        )

    def part_copy(f):
        return pltpu.make_async_remote_copy(
            outward.at[f],
            inward.at[f],
            xs_sem.at[f],
            xr_sem.at[f],
            device_id=partner_tm * n_inp + inp,
            device_id_type=LOGICAL,
        )

    with jax.named_scope("load"):
        for load in loads:
            load.wait()
        gain_b[...] = jnp.broadcast_to(gain[...], (LANES, rows)).T
        feed_b[...] = jnp.broadcast_to(feed[...], (LANES, inputs)).T

    @pl.when(core == 1)
    def _():
        with jax.named_scope("near"):
            inward[0] = jnp.zeros(inward.shape[1:], inward.dtype)
            for f in range(frames):
                filter_frame(f, "near")
                transform_part(f)

    @pl.when(core == 0)
    def _():
        with jax.named_scope("far"):
            split[0] = jnp.zeros(split.shape[1:], split.dtype)
            for f in range(1, frames):
                filter_frame(f, "far")
                transform_part(f)

    with jax.named_scope("barrier"):
        pl.semaphore_wait(barrier, total - 1)

    def ship_whole(c):
        levels = [lax.rem(z + u, n_z) for u in range(n_z)]
        with jax.named_scope(f"ship{c}"):
            ship(send, [c * total + v * owners for v in levels], levels, tm, c, s_sem)

    @pl.when(core == 1)
    def _():
        for g in range(TAPS - 1):
            halo_copy(g).start()
        for f in range(frames):
            part_copy(f).start()

    @pl.when(core == 0)
    def _():
        for f in range(1, frames):
            part_copy(f).start()
        for f in range(frames):
            if f:
                with jax.named_scope(f"halo{f}"):
                    halo_copy(f - 1).wait_recv()
            with jax.named_scope(f"whole{f}"):
                filter_frame(f, "full")
                transform_whole(f)
            if f == PAIR - 1:
                ship_whole(0)

    def steer(i, carry):
        at = pl.ds(pl.multiple_of(i * step_rows, step_rows), step_rows)
        turns = jnp.concatenate([feed_b[at, :]] * (grid.shape[1] // LANES), 1) * grid[...]
        c, s = steer_block(turns, 1.0 / math.sqrt(inputs))
        cosine[at, :] = c
        sine[at, :] = s
        return carry

    for f in range(frames):
        with jax.named_scope(f"part{f}"):
            if f:
                part_copy(f).wait_recv()
            else:

                @pl.when(core == 0)
                def _():
                    part_copy(0).wait_recv()

        with jax.named_scope(f"combine{f}"):
            combine(f)
        if f % PAIR == PAIR - 1:
            c = f // PAIR
            with jax.named_scope(f"shipb{f}"):
                starts = [(c * sides + t) * owners for t in range(sides)]
                ship(send_b, starts, kept, source_tm, c, b_sem)
            if c + 1 < chunks:

                @pl.when(core == 0)
                def _():
                    ship_whole(c + 1)

            if c == 0:
                with jax.named_scope("steer"):
                    lax.fori_loop(0, inputs // step_rows, steer, 0)

    for c in range(chunks - 1):
        with jax.named_scope("arrive"):
            arrived(c)
        with jax.named_scope("arrange"):
            arrange(recv, c * total, n_time, n_inp, spec, turn, spec_t, turn_t)
        width = 256

        def products(j, carry):
            cols = pl.ds(pl.multiple_of(j * width, width), width)
            for ch in range(2):
                right = spec[ch, :, cols]
                sums[ch, 0, :, cols] = jnp.dot(spec_t[ch], right, preferred_element_type=jnp.float32)
                sums[ch, 1, :, cols] = jnp.dot(turn_t[ch], right, preferred_element_type=jnp.float32)
                power[ch, :, cols] = beam_sum(spec, turn, cosine, sine, ch, cols)
            return carry

        with jax.named_scope("products"):
            lax.fori_loop(0, inputs // width, products, 0)
    with jax.named_scope("final"):
        arrived(chunks - 1)

    with jax.named_scope("left"):
        for c in range(chunks):
            some = pl.ds(0, sides * owners - 1)
            pltpu.make_async_copy(send_b.at[some], send_b.at[some], b_sem.at[c]).wait()
        for f in range(1, frames):
            part_copy(f).wait_send()

        @pl.when(core == 1)
        def _():
            part_copy(0).wait_send()
            for g in range(TAPS - 1):
                halo_copy(g).wait_send()

        @pl.when(core == 0)
        def _():
            for c in range(chunks):
                some = pl.ds(0, total - 1)
                pltpu.make_async_copy(send.at[some], send.at[some], s_sem.at[c]).wait()


def exchange(volt, gain, feed, grid, n_time, n_inp):
    rows = volt.shape[0]
    frames = volt.shape[1] // L
    chunks = frames // PAIR
    blocks = chunks * n_time * n_inp
    inputs = feed.shape[1]
    beams = grid.shape[1]
    depth = n_time * 4
    vmem = pl.BlockSpec(memory_space=pltpu.VMEM)
    dma = pltpu.SemaphoreType.DMA
    return pl.pallas_call(
        functools.partial(exchange_kernel, n_time, n_inp),
        name="exchange",
        out_shape=(
            jax.ShapeDtypeStruct((blocks, 8, rows), jnp.bfloat16),
            jax.ShapeDtypeStruct((inputs, beams), jnp.bfloat16),
            jax.ShapeDtypeStruct((inputs, beams), jnp.bfloat16),
            jax.ShapeDtypeStruct((2, 2, inputs, inputs), jnp.float32),
            jax.ShapeDtypeStruct((2, 1, beams), jnp.float32),
        ),
        in_specs=[pl.BlockSpec(memory_space=pltpu.HBM)] * 6,
        out_specs=(vmem,) * 5,
        scratch_shapes=[
            pltpu.VMEM(volt.shape, volt.dtype),
            pltpu.VMEM(gain.shape, gain.dtype),
            pltpu.VMEM((TAPS, L), jnp.float32),
            pltpu.VMEM((2 * CH, L), jnp.bfloat16),
            pltpu.VMEM(feed.shape, feed.dtype),
            pltpu.VMEM(grid.shape, grid.dtype),
            pltpu.VMEM((rows, L), jnp.bfloat16),
            pltpu.VMEM((rows // LANES, 2 * CH * PAIR, LANES), jnp.float32),
            pltpu.VMEM((blocks, 8, rows), jnp.bfloat16),
            pltpu.VMEM((blocks // 2, 8, rows), jnp.bfloat16),
            pltpu.VMEM((rows, (TAPS - 1) * L), jnp.bfloat16),
            pltpu.VMEM((frames, 2 * CH, rows), jnp.float32),
            pltpu.VMEM((frames, n_inp, CH // n_inp, rows), jnp.bfloat16),
            pltpu.VMEM((frames, n_inp, CH // n_inp, rows), jnp.bfloat16),
            pltpu.VMEM((rows, LANES), jnp.float32),
            pltpu.VMEM((inputs, LANES), jnp.int32),
            pltpu.VMEM((2, depth, inputs), jnp.bfloat16),
            pltpu.VMEM((2, depth, inputs), jnp.bfloat16),
            pltpu.VMEM((2, inputs, depth), jnp.bfloat16),
            pltpu.VMEM((2, inputs, depth), jnp.bfloat16),
            dma((chunks,)),
            dma((chunks,)),
            dma((chunks,)),
            dma((TAPS - 1,)),
            dma((TAPS - 1,)),
            dma((frames,)),
            dma((frames,)),
            dma((6,)),
        ],
        compiler_params=pltpu.CompilerParams(collective_id=0, has_side_effects=True, vmem_limit_bytes=30 << 20),
    )(*(pltpu.with_memory_space_constraint(a, pltpu.HBM) for a in (volt, gain, jnp.asarray(window_table()), jnp.asarray(dft_table(n_time, n_inp)), feed, grid)))


def products_kernel(n_time, n_inp, recv, cosine, sine, sums, part, visible, power, spec, turn, spec_t, turn_t):
    ch = pl.program_id(0)
    j = pl.program_id(1)

    @pl.when((ch == 0) & (j == 0))
    def _():
        arrange(recv, n_time * n_inp, n_time, n_inp, spec, turn, spec_t, turn_t)

    width = visible.shape[-1]
    cols = pl.ds(pl.multiple_of(j * width, width), width)
    right = spec[ch, :, cols]
    scale = 1.0 / (4 * n_time)
    for p, left in ((0, spec_t), (1, turn_t)):
        total = sums[ch, p, :, cols] + jnp.dot(left[ch], right, preferred_element_type=jnp.float32)
        visible[0, p] = (total * scale).astype(jnp.bfloat16)
    power[pl.ds(ch, 1), cols] = (part[ch, :, cols] + beam_sum(spec, turn, cosine, sine, ch, cols)) * scale


def products(recv, cosine, sine, sums, part, n_time, n_inp):
    inputs, beams = cosine.shape
    width = 256
    depth = n_time * 4
    vmem = pl.BlockSpec(memory_space=pltpu.VMEM)
    return pl.pallas_call(
        functools.partial(products_kernel, n_time, n_inp),
        name="products",
        grid=(2, inputs // width),
        out_shape=(
            jax.ShapeDtypeStruct((2, 2, inputs, inputs), jnp.bfloat16),
            jax.ShapeDtypeStruct((2, beams), jnp.float32),
        ),
        in_specs=[vmem] * 5,
        out_specs=(
            pl.BlockSpec((1, 2, inputs, width), lambda c, j: (c, 0, 0, j)),
            vmem,
        ),
        scratch_shapes=[
            pltpu.VMEM((2, depth, inputs), jnp.bfloat16),
            pltpu.VMEM((2, depth, inputs), jnp.bfloat16),
            pltpu.VMEM((2, inputs, depth), jnp.bfloat16),
            pltpu.VMEM((2, inputs, depth), jnp.bfloat16),
        ],
        compiler_params=pltpu.CompilerParams(vmem_limit_bytes=12 << 20),
    )(recv, cosine, sine, sums, part)


def on_device(voltages, input_gain, input_feed, beam_grid):
    n_time = lax.axis_size("tm")
    n_inp = lax.axis_size("inp")
    got = exchange(voltages, input_gain[None], input_feed[None], beam_grid[None], n_time, n_inp)
    return products(*got, n_time, n_inp)


def solution(mesh):
    return jax.shard_map(
        on_device,
        mesh=mesh,
        in_specs=(P("inp", "tm"), P("inp"), P(), P()),
        out_specs=(P(("tm", "inp"), None, None, None), P(("tm", "inp"), None)),
        check_vma=False,
    )
```

```python
import functools
import math

import jax
import jax.numpy as jnp
import numpy as np
from jax import lax
from jax.experimental import pallas as pl
from jax.experimental.pallas import tpu as pltpu
from jax.sharding import PartitionSpec as P

LOGICAL = pl.DeviceIdType.LOGICAL
L = 1024
CH = 512
TAPS = 4
GRID = 512
LANES = 128
PAIR = 2


def window_table():
    span = TAPS * L
    pos = np.arange(span).astype(np.float64)
    sinc_part = np.sinc((pos - span / 2) / L)
    hann_part = 0.5 - 0.5 * np.cos(2.0 * np.pi * pos / span)
    return (sinc_part * hann_part).reshape(TAPS, L).astype(np.float32)


def dft_table(n_time, n_inp):
    step = np.arange(CH)[:, None] * np.arange(L)[None, :] % L
    radians = 2.0 * np.pi * step / L
    rows = np.stack([np.cos(radians), -np.sin(radians)], 1) / math.sqrt(L)
    rows = rows.reshape(n_time // 4, 2, 2, n_inp, -1, L).transpose(3, 1, 0, 2, 4, 5)
    return rows.reshape(2 * CH, L).astype(jnp.bfloat16)


def steer_block(phase, factor):
    phase = phase & (GRID - 1)
    turned = phase + GRID // 8
    quarter = (turned >> 7) & 3
    rest = (turned & 127) - GRID // 8
    x = rest.astype(jnp.float32) * (2.0 * math.pi / GRID)
    y = x * x
    sine = x * (1.0 + y * (-1.0 / 6 + y * (1.0 / 120 + y * (-1.0 / 5040 + y * (1.0 / 362880)))))
    cosine = 1.0 + y * (-0.5 + y * (1.0 / 24 + y * (-1.0 / 720 + y * (1.0 / 40320))))
    swap = (quarter & 1) == 1
    c_sign = jnp.where((quarter == 1) | (quarter == 2), -factor, factor)
    s_sign = jnp.where(quarter >= 2, factor, -factor)
    c = jnp.where(swap, sine, cosine) * c_sign
    s = jnp.where(swap, cosine, sine) * s_sign
    return c.astype(jnp.bfloat16), s.astype(jnp.bfloat16)


def arrange(recv, first, n_time, n_inp, spec, turn, spec_t, turn_t):
    width = recv.shape[2]
    half = n_time // 2
    rows = half * 8
    row = lax.broadcasted_iota(jnp.int32, (half, 8, width), 1)
    low = row < 4
    real = (row & 2) == 0
    for g in range(n_inp):
        lanes = slice(g * width, (g + 1) * width)
        got = recv[first + g * n_time : first + (g + 1) * n_time].astype(jnp.float32).reshape(half, 2, 8, width)
        even, odd = got[:, 0], got[:, 1]
        for ch in range(2):
            if ch == 0:
                y = jnp.where(low, even, pltpu.roll(odd, 4, 1))
            else:
                y = jnp.where(low, pltpu.roll(even, 4, 1), odd)
            z = jnp.where(real, pltpu.roll(y, 6, 1), -pltpu.roll(y, 2, 1))
            y = y.reshape(rows, width)
            z = z.reshape(rows, width)
            spec[ch, :, lanes] = y.astype(jnp.bfloat16)
            turn[ch, :, lanes] = z.astype(jnp.bfloat16)
            spec_t[ch, lanes, :] = y.T.astype(jnp.bfloat16)
            turn_t[ch, lanes, :] = z.T.astype(jnp.bfloat16)


def beam_sum(spec, turn, cosine, sine, ch, cols):
    beams = jnp.dot(spec[ch], cosine[:, cols], preferred_element_type=jnp.float32) + jnp.dot(
        turn[ch], sine[:, cols], preferred_element_type=jnp.float32
    )
    return jnp.sum(beams * beams, axis=0, keepdims=True)


def exchange_kernel(
    n_time,
    n_inp,
    volt_h,
    gain_h,
    window_h,
    table_h,
    feed_h,
    grid_h,
    recv,
    cosine,
    sine,
    sums,
    power,
    volt,
    gain,
    window,
    table,
    feed,
    grid,
    filt,
    wide,
    send,
    send_b,
    halo,
    split,
    outward,
    inward,
    gain_b,
    feed_b,
    spec,
    turn,
    spec_t,
    turn_t,
    s_sem,
    b_sem,
    r_sem,
    hs_sem,
    hr_sem,
    xs_sem,
    xr_sem,
    in_sem,
):
    total = n_time * n_inp
    rows = volt.shape[0]
    inputs = feed.shape[1]
    frames = volt.shape[1] // L
    chunks = frames // PAIR
    n_yx, n_z = n_time // 4, 2 * n_inp
    sides = n_z // 2
    group = 2 * CH // n_z
    owners = group // 4
    tm = lax.axis_index("tm")
    inp = lax.axis_index("inp")
    me = tm * n_inp + inp
    core = lax.rem(tm, 2)
    z_lo = lax.rem(tm // 2, 2)
    yx = tm // 4
    z = 2 * inp + z_lo
    way = 2 * z_lo - 1
    kept = [lax.rem(z + way * t + n_z, n_z) for t in range(sides)]
    given = [lax.rem(z - way * (t + 1) + n_z, n_z) for t in range(sides)]
    partner_tm = lax.rem(tm + 2 * core - 1 + n_time, n_time)
    source_tm = lax.rem(tm + core - 1 + n_time, n_time)
    barrier = pltpu.get_barrier_semaphore()
    loads = [
        pltpu.make_async_copy(there, here, in_sem.at[i])
        for i, (there, here) in enumerate(
            ((volt_h, volt), (window_h, window), (gain_h, gain), (feed_h, feed), (grid_h, grid), (table_h, table))
        )
    ]
    for load in loads:
        load.start()

    def greet(d, carry):
        pl.semaphore_signal(barrier, inc=1, device_id=d, device_id_type=LOGICAL)
        return carry

    plane = 4 * n_inp

    def greet_plane(row, carry):
        for i in range(plane):
            greet(row * plane + i, carry)
        return carry

    with jax.named_scope("greet"):
        lax.fori_loop(yx + 1, n_yx, greet_plane, 0)
        lax.fori_loop(0, yx, greet_plane, 0)
        lax.fori_loop(me + 1, (yx + 1) * plane, greet, 0)
        lax.fori_loop(yx * plane, me, greet, 0)

    step_rows = 16

    def filter_frame(f, kind):
        def one(i, carry):
            at = pl.ds(pl.multiple_of(i * step_rows, step_rows), step_rows)
            summed = None
            for tap in range(TAPS):
                g = f + tap
                if (kind == "near" and g >= frames) or (kind == "far" and g < frames):
                    continue
                if kind == "full" and g >= frames:
                    piece = halo[at, (g - frames) * L : (g - frames + 1) * L]
                else:
                    piece = volt[at, g % frames * L : (g % frames + 1) * L]
                term = piece.astype(jnp.float32) * window[tap : tap + 1, :]
                summed = term if summed is None else summed + term
            scale = gain_b[at, :]
            if kind == "far":
                scale = jnp.where(tm == 0, 0.0, scale)
            scale = jnp.concatenate([scale] * (L // LANES), 1)
            filt[at, :] = (summed * scale).astype(jnp.bfloat16)
            return carry

        lax.fori_loop(0, rows // step_rows, one, 0)

    block = 256

    def spectrum(b):
        return lax.dot_general(
            table[pl.ds(b * block, block), :], filt[...], (((1,), (1,)), ((), ())), preferred_element_type=jnp.float32
        )

    def pack(part, place, first, count, target, at):
        for h in range(rows // LANES):
            wide[h, pl.ds(first * PAIR + place, count, stride=PAIR), :] = part[:, h * LANES : (h + 1) * LANES]
        if place == PAIR - 1:
            n = count * PAIR // 8
            for h in range(rows // LANES):
                ready = wide[h, first * PAIR : (first + count) * PAIR, :].astype(jnp.bfloat16).reshape(n, 8, LANES)
                target[at : at + n, :, h * LANES : (h + 1) * LANES] = ready

    def transform_whole(f):
        for b in range(2 * CH // block):
            pack(spectrum(b), f % PAIR, b * block, block, send, f // PAIR * total + b * block // 4)

    def transform_part(f):
        for b in range(2 * CH // block):
            split[f, b * block : (b + 1) * block, :] = spectrum(b)
        for t in range(sides):
            at = pl.ds(pl.multiple_of(given[t] * group, group), group)
            outward[f, t] = split[f, at, :].astype(jnp.bfloat16)

    def combine(f):
        for t in range(sides):
            at = pl.ds(pl.multiple_of(kept[t] * group, group), group)
            part = split[f, at, :] + inward[f, t].astype(jnp.float32)
            pack(part, f % PAIR, t * group, group, send_b, f // PAIR * sides * owners + t * owners)

    def ship(source, starts, levels, source_tm, c, sem):
        slot = c * total + inp * n_time + source_tm
        firsts = [lax.rem(v, 2) * 2 * n_inp + v // 2 for v in levels]

        def copy(row, i, side):
            pltpu.make_async_remote_copy(
                source.at[starts[i] + row * 2 + side],
                recv.at[slot],
                sem.at[c],
                r_sem.at[c],
                device_id=row * 4 * n_inp + firsts[i] + side * n_inp,
                device_id_type=LOGICAL,
            ).start()

        def one(row, carry):
            for i in range(len(levels)):
                for side in range(2):
                    copy(row, i, side)
            return carry

        lax.fori_loop(yx + 1, n_yx, one, 0)
        copy(yx, 0, 1 - core)
        for i in range(1, len(levels)):
            for side in range(2):
                copy(yx, i, side)
        lax.fori_loop(0, yx, one, 0)
        pltpu.make_async_copy(source.at[starts[0] + yx * 2 + core], recv.at[slot], r_sem.at[c]).start()

    def arrived(c):
        some = pl.ds(c * total, total)
        pltpu.make_async_copy(recv.at[some], recv.at[some], r_sem.at[c]).wait()

    def halo_copy(g):
        cols = pl.ds(g * L, L)
        return pltpu.make_async_remote_copy(
            volt.at[:, cols],
            halo.at[:, cols],
            hs_sem.at[g],
            hr_sem.at[g],
            device_id=me - n_inp,
            device_id_type=LOGICAL,
        )

    def part_copy(f):
        return pltpu.make_async_remote_copy(
            outward.at[f],
            inward.at[f],
            xs_sem.at[f],
            xr_sem.at[f],
            device_id=partner_tm * n_inp + inp,
            device_id_type=LOGICAL,
        )

    with jax.named_scope("load"):
        for load in loads:
            load.wait()
        gain_b[...] = jnp.broadcast_to(gain[...], (LANES, rows)).T
        feed_b[...] = jnp.broadcast_to(feed[...], (LANES, inputs)).T

    def meet():
        with jax.named_scope("barrier"):
            pl.semaphore_wait(barrier, total - 1)

    @pl.when(core == 1)
    def _():
        inward[0] = jnp.zeros(inward.shape[1:], inward.dtype)
        for f in range(frames):
            with jax.named_scope(f"near{f}"):
                filter_frame(f, "near")
                transform_part(f)
            if f == PAIR - 1:
                meet()
                for g in range(TAPS - 1):
                    halo_copy(g).start()
                for done in range(PAIR):
                    part_copy(done).start()
            elif f >= PAIR:
                part_copy(f).start()

    @pl.when(core == 0)
    def _():
        with jax.named_scope("far"):
            split[0] = jnp.zeros(split.shape[1:], split.dtype)
            for f in range(1, frames):
                filter_frame(f, "far")
                transform_part(f)
        meet()
        for f in range(1, frames):
            part_copy(f).start()
        levels = [lax.rem(z + u, n_z) for u in range(n_z)]
        for f in range(frames):
            if f:
                with jax.named_scope(f"halo{f}"):
                    halo_copy(f - 1).wait_recv()
            with jax.named_scope(f"whole{f}"):
                filter_frame(f, "full")
                transform_whole(f)
            if f % PAIR == PAIR - 1:
                c = f // PAIR
                with jax.named_scope(f"ship{f}"):
                    ship(send, [c * total + v * owners for v in levels], levels, tm, c, s_sem)

    def steer(i, carry):
        at = pl.ds(pl.multiple_of(i * step_rows, step_rows), step_rows)
        turns = jnp.concatenate([feed_b[at, :]] * (grid.shape[1] // LANES), 1) * grid[...]
        c, s = steer_block(turns, 1.0 / math.sqrt(inputs))
        cosine[at, :] = c
        sine[at, :] = s
        return carry

    with jax.named_scope("steer"):
        lax.fori_loop(0, inputs // step_rows, steer, 0)

    for f in range(frames):
        with jax.named_scope(f"part{f}"):
            if f:
                part_copy(f).wait_recv()
            else:

                @pl.when(core == 0)
                def _():
                    part_copy(0).wait_recv()

        with jax.named_scope(f"combine{f}"):
            combine(f)
        if f % PAIR == PAIR - 1:
            c = f // PAIR
            with jax.named_scope(f"shipb{f}"):
                starts = [(c * sides + t) * owners for t in range(sides)]
                ship(send_b, starts, kept, source_tm, c, b_sem)

    for c in range(chunks - 1):
        with jax.named_scope("arrive"):
            arrived(c)
        with jax.named_scope("arrange"):
            arrange(recv, c * total, n_time, n_inp, spec, turn, spec_t, turn_t)
        width = 256

        def products(j, carry):
            cols = pl.ds(pl.multiple_of(j * width, width), width)
            for ch in range(2):
                right = spec[ch, :, cols]
                sums[ch, 0, :, cols] = jnp.dot(spec_t[ch], right, preferred_element_type=jnp.float32)
                sums[ch, 1, :, cols] = jnp.dot(turn_t[ch], right, preferred_element_type=jnp.float32)
                power[ch, :, cols] = beam_sum(spec, turn, cosine, sine, ch, cols)
            return carry

        with jax.named_scope("products"):
            lax.fori_loop(0, inputs // width, products, 0)
    with jax.named_scope("final"):
        arrived(chunks - 1)

    with jax.named_scope("left"):
        for c in range(chunks):
            some = pl.ds(0, sides * owners - 1)
            pltpu.make_async_copy(send_b.at[some], send_b.at[some], b_sem.at[c]).wait()
        for f in range(1, frames):
            part_copy(f).wait_send()

        @pl.when(core == 1)
        def _():
            part_copy(0).wait_send()
            for g in range(TAPS - 1):
                halo_copy(g).wait_send()

        @pl.when(core == 0)
        def _():
            for c in range(chunks):
                some = pl.ds(0, total - 1)
                pltpu.make_async_copy(send.at[some], send.at[some], s_sem.at[c]).wait()


def exchange(volt, gain, feed, grid, n_time, n_inp):
    rows = volt.shape[0]
    frames = volt.shape[1] // L
    chunks = frames // PAIR
    blocks = chunks * n_time * n_inp
    inputs = feed.shape[1]
    beams = grid.shape[1]
    depth = n_time * 4
    vmem = pl.BlockSpec(memory_space=pltpu.VMEM)
    dma = pltpu.SemaphoreType.DMA
    return pl.pallas_call(
        functools.partial(exchange_kernel, n_time, n_inp),
        name="exchange",
        out_shape=(
            jax.ShapeDtypeStruct((blocks, 8, rows), jnp.bfloat16),
            jax.ShapeDtypeStruct((inputs, beams), jnp.bfloat16),
            jax.ShapeDtypeStruct((inputs, beams), jnp.bfloat16),
            jax.ShapeDtypeStruct((2, 2, inputs, inputs), jnp.float32),
            jax.ShapeDtypeStruct((2, 1, beams), jnp.float32),
        ),
        in_specs=[pl.BlockSpec(memory_space=pltpu.HBM)] * 6,
        out_specs=(vmem,) * 5,
        scratch_shapes=[
            pltpu.VMEM(volt.shape, volt.dtype),
            pltpu.VMEM(gain.shape, gain.dtype),
            pltpu.VMEM((TAPS, L), jnp.float32),
            pltpu.VMEM((2 * CH, L), jnp.bfloat16),
            pltpu.VMEM(feed.shape, feed.dtype),
            pltpu.VMEM(grid.shape, grid.dtype),
            pltpu.VMEM((rows, L), jnp.bfloat16),
            pltpu.VMEM((rows // LANES, 2 * CH * PAIR, LANES), jnp.float32),
            pltpu.VMEM((blocks, 8, rows), jnp.bfloat16),
            pltpu.VMEM((blocks // 2, 8, rows), jnp.bfloat16),
            pltpu.VMEM((rows, (TAPS - 1) * L), jnp.bfloat16),
            pltpu.VMEM((frames, 2 * CH, rows), jnp.float32),
            pltpu.VMEM((frames, n_inp, CH // n_inp, rows), jnp.bfloat16),
            pltpu.VMEM((frames, n_inp, CH // n_inp, rows), jnp.bfloat16),
            pltpu.VMEM((rows, LANES), jnp.float32),
            pltpu.VMEM((inputs, LANES), jnp.int32),
            pltpu.VMEM((2, depth, inputs), jnp.bfloat16),
            pltpu.VMEM((2, depth, inputs), jnp.bfloat16),
            pltpu.VMEM((2, inputs, depth), jnp.bfloat16),
            pltpu.VMEM((2, inputs, depth), jnp.bfloat16),
            dma((chunks,)),
            dma((chunks,)),
            dma((chunks,)),
            dma((TAPS - 1,)),
            dma((TAPS - 1,)),
            dma((frames,)),
            dma((frames,)),
            dma((6,)),
        ],
        compiler_params=pltpu.CompilerParams(collective_id=0, has_side_effects=True, vmem_limit_bytes=30 << 20),
    )(*(pltpu.with_memory_space_constraint(a, pltpu.HBM) for a in (volt, gain, jnp.asarray(window_table()), jnp.asarray(dft_table(n_time, n_inp)), feed, grid)))


def products_kernel(n_time, n_inp, recv, cosine, sine, sums, part, visible, power, spec, turn, spec_t, turn_t):
    ch = pl.program_id(0)
    j = pl.program_id(1)

    @pl.when((ch == 0) & (j == 0))
    def _():
        arrange(recv, n_time * n_inp, n_time, n_inp, spec, turn, spec_t, turn_t)

    width = visible.shape[-1]
    cols = pl.ds(pl.multiple_of(j * width, width), width)
    right = spec[ch, :, cols]
    scale = 1.0 / (4 * n_time)
    for p, left in ((0, spec_t), (1, turn_t)):
        total = sums[ch, p, :, cols] + jnp.dot(left[ch], right, preferred_element_type=jnp.float32)
        visible[0, p] = (total * scale).astype(jnp.bfloat16)
    power[pl.ds(ch, 1), cols] = (part[ch, :, cols] + beam_sum(spec, turn, cosine, sine, ch, cols)) * scale


def products(recv, cosine, sine, sums, part, n_time, n_inp):
    inputs, beams = cosine.shape
    width = 512
    depth = n_time * 4
    vmem = pl.BlockSpec(memory_space=pltpu.VMEM)
    return pl.pallas_call(
        functools.partial(products_kernel, n_time, n_inp),
        name="products",
        grid=(2, inputs // width),
        out_shape=(
            jax.ShapeDtypeStruct((2, 2, inputs, inputs), jnp.bfloat16),
            jax.ShapeDtypeStruct((2, beams), jnp.float32),
        ),
        in_specs=[vmem] * 5,
        out_specs=(
            pl.BlockSpec((1, 2, inputs, width), lambda c, j: (c, 0, 0, j)),
            vmem,
        ),
        scratch_shapes=[
            pltpu.VMEM((2, depth, inputs), jnp.bfloat16),
            pltpu.VMEM((2, depth, inputs), jnp.bfloat16),
            pltpu.VMEM((2, inputs, depth), jnp.bfloat16),
            pltpu.VMEM((2, inputs, depth), jnp.bfloat16),
        ],
        compiler_params=pltpu.CompilerParams(vmem_limit_bytes=12 << 20),
    )(recv, cosine, sine, sums, part)


def on_device(voltages, input_gain, input_feed, beam_grid):
    n_time = lax.axis_size("tm")
    n_inp = lax.axis_size("inp")
    got = exchange(voltages, input_gain[None], input_feed[None], beam_grid[None], n_time, n_inp)
    return products(*got, n_time, n_inp)


def solution(mesh):
    return jax.shard_map(
        on_device,
        mesh=mesh,
        in_specs=(P("inp", "tm"), P("inp"), P(), P()),
        out_specs=(P(("tm", "inp"), None, None, None), P(("tm", "inp"), None)),
        check_vma=False,
    )
```

```python
import functools
import math

import jax
import jax.numpy as jnp
import numpy as np
from jax import lax
from jax.experimental import pallas as pl
from jax.experimental.pallas import tpu as pltpu
from jax.sharding import PartitionSpec as P

LOGICAL = pl.DeviceIdType.LOGICAL
L = 1024
CH = 512
TAPS = 4
GRID = 512
LANES = 128
PAIR = 2


def window_table():
    span = TAPS * L
    pos = np.arange(span).astype(np.float64)
    sinc_part = np.sinc((pos - span / 2) / L)
    hann_part = 0.5 - 0.5 * np.cos(2.0 * np.pi * pos / span)
    return (sinc_part * hann_part).reshape(TAPS, L).astype(np.float32)


def dft_table(n_time, n_inp):
    step = np.arange(CH)[:, None] * np.arange(L)[None, :] % L
    radians = 2.0 * np.pi * step / L
    rows = np.stack([np.cos(radians), -np.sin(radians)], 1) / math.sqrt(L)
    rows = rows.reshape(n_time // 4, 2, 2, n_inp, -1, L).transpose(3, 1, 0, 2, 4, 5)
    return rows.reshape(2 * CH, L).astype(jnp.bfloat16)


def steer_block(phase, factor):
    phase = phase & (GRID - 1)
    turned = phase + GRID // 8
    quarter = (turned >> 7) & 3
    rest = (turned & 127) - GRID // 8
    x = rest.astype(jnp.float32) * (2.0 * math.pi / GRID)
    y = x * x
    sine = x * (1.0 + y * (-1.0 / 6 + y * (1.0 / 120 + y * (-1.0 / 5040 + y * (1.0 / 362880)))))
    cosine = 1.0 + y * (-0.5 + y * (1.0 / 24 + y * (-1.0 / 720 + y * (1.0 / 40320))))
    swap = (quarter & 1) == 1
    c_sign = jnp.where((quarter == 1) | (quarter == 2), -factor, factor)
    s_sign = jnp.where(quarter >= 2, factor, -factor)
    c = jnp.where(swap, sine, cosine) * c_sign
    s = jnp.where(swap, cosine, sine) * s_sign
    return c.astype(jnp.bfloat16), s.astype(jnp.bfloat16)


def arrange(recv, first, n_time, n_inp, spec, turn, spec_t, turn_t):
    width = recv.shape[2]
    half = n_time // 2
    rows = half * 8
    row = lax.broadcasted_iota(jnp.int32, (half, 8, width), 1)
    low = row < 4
    real = (row & 2) == 0
    for g in range(n_inp):
        lanes = slice(g * width, (g + 1) * width)
        got = recv[first + g * n_time : first + (g + 1) * n_time].astype(jnp.float32).reshape(half, 2, 8, width)
        even, odd = got[:, 0], got[:, 1]
        for ch in range(2):
            if ch == 0:
                y = jnp.where(low, even, pltpu.roll(odd, 4, 1))
            else:
                y = jnp.where(low, pltpu.roll(even, 4, 1), odd)
            z = jnp.where(real, pltpu.roll(y, 6, 1), -pltpu.roll(y, 2, 1))
            y = y.reshape(rows, width)
            z = z.reshape(rows, width)
            spec[ch, :, lanes] = y.astype(jnp.bfloat16)
            turn[ch, :, lanes] = z.astype(jnp.bfloat16)
            spec_t[ch, lanes, :] = y.T.astype(jnp.bfloat16)
            turn_t[ch, lanes, :] = z.T.astype(jnp.bfloat16)


def beam_sum(spec, turn, cosine, sine, ch, cols):
    beams = jnp.dot(spec[ch], cosine[:, cols], preferred_element_type=jnp.float32) + jnp.dot(
        turn[ch], sine[:, cols], preferred_element_type=jnp.float32
    )
    return jnp.sum(beams * beams, axis=0, keepdims=True)


def exchange_kernel(
    n_time,
    n_inp,
    volt_h,
    gain_h,
    window_h,
    table_h,
    feed_h,
    grid_h,
    recv,
    cosine,
    sine,
    sums,
    power,
    volt,
    gain,
    window,
    table,
    feed,
    grid,
    filt,
    wide,
    send,
    send_b,
    halo,
    split,
    outward,
    inward,
    gain_b,
    feed_b,
    spec,
    turn,
    spec_t,
    turn_t,
    s_sem,
    b_sem,
    r_sem,
    hs_sem,
    hr_sem,
    xs_sem,
    xr_sem,
    in_sem,
):
    total = n_time * n_inp
    rows = volt.shape[0]
    inputs = feed.shape[1]
    frames = volt.shape[1] // L
    chunks = frames // PAIR
    n_yx, n_z = n_time // 4, 2 * n_inp
    sides = n_z // 2
    group = 2 * CH // n_z
    owners = group // 4
    tm = lax.axis_index("tm")
    inp = lax.axis_index("inp")
    me = tm * n_inp + inp
    core = lax.rem(tm, 2)
    z_lo = lax.rem(tm // 2, 2)
    yx = tm // 4
    z = 2 * inp + z_lo
    way = 2 * z_lo - 1
    kept = [lax.rem(z + way * t + n_z, n_z) for t in range(sides)]
    given = [lax.rem(z - way * (t + 1) + n_z, n_z) for t in range(sides)]
    partner_tm = lax.rem(tm + 2 * core - 1 + n_time, n_time)
    source_tm = lax.rem(tm + core - 1 + n_time, n_time)
    barrier = pltpu.get_barrier_semaphore()
    loads = [
        pltpu.make_async_copy(there, here, in_sem.at[i])
        for i, (there, here) in enumerate(
            ((volt_h, volt), (window_h, window), (gain_h, gain), (feed_h, feed), (grid_h, grid), (table_h, table))
        )
    ]
    for load in loads:
        load.start()

    def greet(d, carry):
        pl.semaphore_signal(barrier, inc=1, device_id=d, device_id_type=LOGICAL)
        return carry

    plane = 4 * n_inp

    def greet_plane(row, carry):
        for i in range(plane):
            greet(row * plane + i, carry)
        return carry

    with jax.named_scope("greet"):
        lax.fori_loop(yx + 1, n_yx, greet_plane, 0)
        lax.fori_loop(0, yx, greet_plane, 0)
        lax.fori_loop(me + 1, (yx + 1) * plane, greet, 0)
        lax.fori_loop(yx * plane, me, greet, 0)

    step_rows = 16

    def filter_frame(f, kind):
        def one(i, carry):
            at = pl.ds(pl.multiple_of(i * step_rows, step_rows), step_rows)
            summed = None
            for tap in range(TAPS):
                g = f + tap
                if (kind == "near" and g >= frames) or (kind == "far" and g < frames):
                    continue
                if kind == "full" and g >= frames:
                    piece = halo[at, (g - frames) * L : (g - frames + 1) * L]
                else:
                    piece = volt[at, g % frames * L : (g % frames + 1) * L]
                term = piece.astype(jnp.float32) * window[tap : tap + 1, :]
                summed = term if summed is None else summed + term
            scale = gain_b[at, :]
            if kind == "far":
                scale = jnp.where(tm == 0, 0.0, scale)
            scale = jnp.concatenate([scale] * (L // LANES), 1)
            filt[at, :] = (summed * scale).astype(jnp.bfloat16)
            return carry

        lax.fori_loop(0, rows // step_rows, one, 0)

    block = 256

    def spectrum(b):
        return lax.dot_general(
            table[pl.ds(b * block, block), :], filt[...], (((1,), (1,)), ((), ())), preferred_element_type=jnp.float32
        )

    def pack(part, place, first, count, target, at):
        for h in range(rows // LANES):
            wide[h, pl.ds(first * PAIR + place, count, stride=PAIR), :] = part[:, h * LANES : (h + 1) * LANES]
        if place == PAIR - 1:
            n = count * PAIR // 8
            for h in range(rows // LANES):
                ready = wide[h, first * PAIR : (first + count) * PAIR, :].astype(jnp.bfloat16).reshape(n, 8, LANES)
                target[at : at + n, :, h * LANES : (h + 1) * LANES] = ready

    def transform_whole(f):
        for b in range(2 * CH // block):
            pack(spectrum(b), f % PAIR, b * block, block, send, f // PAIR * total + b * block // 4)

    def transform_part(f):
        for b in range(2 * CH // block):
            split[f, b * block : (b + 1) * block, :] = spectrum(b)
        for t in range(sides):
            at = pl.ds(pl.multiple_of(given[t] * group, group), group)
            outward[f, t] = split[f, at, :].astype(jnp.bfloat16)

    def combine(f):
        for t in range(sides):
            at = pl.ds(pl.multiple_of(kept[t] * group, group), group)
            part = split[f, at, :] + inward[f, t].astype(jnp.float32)
            pack(part, f % PAIR, t * group, group, send_b, f // PAIR * sides * owners + t * owners)

    def ship(source, starts, levels, source_tm, c, sem):
        slot = c * total + inp * n_time + source_tm
        firsts = [lax.rem(v, 2) * 2 * n_inp + v // 2 for v in levels]

        def copy(row, i, side):
            pltpu.make_async_remote_copy(
                source.at[starts[i] + row * 2 + side],
                recv.at[slot],
                sem.at[c],
                r_sem.at[c],
                device_id=row * 4 * n_inp + firsts[i] + side * n_inp,
                device_id_type=LOGICAL,
            ).start()

        def one(row, carry):
            for i in range(len(levels)):
                for side in range(2):
                    copy(row, i, side)
            return carry

        lax.fori_loop(yx + 1, n_yx, one, 0)
        copy(yx, 0, 1 - core)
        for i in range(1, len(levels)):
            for side in range(2):
                copy(yx, i, side)
        lax.fori_loop(0, yx, one, 0)
        pltpu.make_async_copy(source.at[starts[0] + yx * 2 + core], recv.at[slot], r_sem.at[c]).start()

    def arrived(c):
        some = pl.ds(c * total, total)
        pltpu.make_async_copy(recv.at[some], recv.at[some], r_sem.at[c]).wait()

    def halo_copy(g):
        cols = pl.ds(g * L, L)
        return pltpu.make_async_remote_copy(
            volt.at[:, cols],
            halo.at[:, cols],
            hs_sem.at[g],
            hr_sem.at[g],
            device_id=me - n_inp,
            device_id_type=LOGICAL,
        )

    def part_copy(f):
        return pltpu.make_async_remote_copy(
            outward.at[f],
            inward.at[f],
            xs_sem.at[f],
            xr_sem.at[f],
            device_id=partner_tm * n_inp + inp,
            device_id_type=LOGICAL,
        )

    with jax.named_scope("load"):
        for load in loads[:3]:
            load.wait()
        gain_b[...] = jnp.broadcast_to(gain[...], (LANES, rows)).T

    def meet():
        with jax.named_scope("barrier"):
            pl.semaphore_wait(barrier, total - 1)

    @pl.when(core == 1)
    def _():
        inward[0] = jnp.zeros(inward.shape[1:], inward.dtype)
        for f in range(frames):
            with jax.named_scope(f"near{f}"):
                filter_frame(f, "near")
                if f == 0:
                    loads[5].wait()
                transform_part(f)
            if f == PAIR - 1:
                meet()
                for g in range(TAPS - 1):
                    halo_copy(g).start()
                for done in range(PAIR):
                    part_copy(done).start()
            elif f >= PAIR:
                part_copy(f).start()

    @pl.when(core == 0)
    def _():
        with jax.named_scope("far"):
            split[0] = jnp.zeros(split.shape[1:], split.dtype)
            for f in range(1, frames):
                filter_frame(f, "far")
                if f == 1:
                    loads[5].wait()
                transform_part(f)
        meet()
        for f in range(1, frames):
            part_copy(f).start()
        levels = [lax.rem(z + u, n_z) for u in range(n_z)]
        for f in range(frames):
            if f:
                with jax.named_scope(f"halo{f}"):
                    halo_copy(f - 1).wait_recv()
            with jax.named_scope(f"whole{f}"):
                filter_frame(f, "full")
                transform_whole(f)
            if f % PAIR == PAIR - 1:
                c = f // PAIR
                with jax.named_scope(f"ship{f}"):
                    ship(send, [c * total + v * owners for v in levels], levels, tm, c, s_sem)

    def steer(i, carry):
        at = pl.ds(pl.multiple_of(i * step_rows, step_rows), step_rows)
        turns = jnp.concatenate([feed_b[at, :]] * (grid.shape[1] // LANES), 1) * grid[...]
        c, s = steer_block(turns, 1.0 / math.sqrt(inputs))
        cosine[at, :] = c
        sine[at, :] = s
        return carry

    with jax.named_scope("steer"):
        for load in loads[3:5]:
            load.wait()
        feed_b[...] = jnp.broadcast_to(feed[...], (LANES, inputs)).T
        lax.fori_loop(0, inputs // step_rows, steer, 0)

    for f in range(frames):
        with jax.named_scope(f"part{f}"):
            if f:
                part_copy(f).wait_recv()
            else:

                @pl.when(core == 0)
                def _():
                    part_copy(0).wait_recv()

        with jax.named_scope(f"combine{f}"):
            combine(f)
        if f % PAIR == PAIR - 1:
            c = f // PAIR
            with jax.named_scope(f"shipb{f}"):
                starts = [(c * sides + t) * owners for t in range(sides)]
                ship(send_b, starts, kept, source_tm, c, b_sem)

    for c in range(chunks - 1):
        with jax.named_scope("arrive"):
            arrived(c)
        with jax.named_scope("arrange"):
            arrange(recv, c * total, n_time, n_inp, spec, turn, spec_t, turn_t)
        width = 256

        def products(j, carry):
            cols = pl.ds(pl.multiple_of(j * width, width), width)
            for ch in range(2):
                right = spec[ch, :, cols]
                sums[ch, 0, :, cols] = jnp.dot(spec_t[ch], right, preferred_element_type=jnp.float32)
                sums[ch, 1, :, cols] = jnp.dot(turn_t[ch], right, preferred_element_type=jnp.float32)
                power[ch, :, cols] = beam_sum(spec, turn, cosine, sine, ch, cols)
            return carry

        with jax.named_scope("products"):
            lax.fori_loop(0, inputs // width, products, 0)
    with jax.named_scope("final"):
        arrived(chunks - 1)

    with jax.named_scope("left"):
        for c in range(chunks):
            some = pl.ds(0, sides * owners - 1)
            pltpu.make_async_copy(send_b.at[some], send_b.at[some], b_sem.at[c]).wait()
        for f in range(1, frames):
            part_copy(f).wait_send()

        @pl.when(core == 1)
        def _():
            part_copy(0).wait_send()
            for g in range(TAPS - 1):
                halo_copy(g).wait_send()

        @pl.when(core == 0)
        def _():
            for c in range(chunks):
                some = pl.ds(0, total - 1)
                pltpu.make_async_copy(send.at[some], send.at[some], s_sem.at[c]).wait()


def exchange(volt, gain, feed, grid, n_time, n_inp):
    rows = volt.shape[0]
    frames = volt.shape[1] // L
    chunks = frames // PAIR
    blocks = chunks * n_time * n_inp
    inputs = feed.shape[1]
    beams = grid.shape[1]
    depth = n_time * 4
    vmem = pl.BlockSpec(memory_space=pltpu.VMEM)
    dma = pltpu.SemaphoreType.DMA
    return pl.pallas_call(
        functools.partial(exchange_kernel, n_time, n_inp),
        name="exchange",
        out_shape=(
            jax.ShapeDtypeStruct((blocks, 8, rows), jnp.bfloat16),
            jax.ShapeDtypeStruct((inputs, beams), jnp.bfloat16),
            jax.ShapeDtypeStruct((inputs, beams), jnp.bfloat16),
            jax.ShapeDtypeStruct((2, 2, inputs, inputs), jnp.float32),
            jax.ShapeDtypeStruct((2, 1, beams), jnp.float32),
        ),
        in_specs=[pl.BlockSpec(memory_space=pltpu.HBM)] * 6,
        out_specs=(vmem,) * 5,
        scratch_shapes=[
            pltpu.VMEM(volt.shape, volt.dtype),
            pltpu.VMEM(gain.shape, gain.dtype),
            pltpu.VMEM((TAPS, L), jnp.float32),
            pltpu.VMEM((2 * CH, L), jnp.bfloat16),
            pltpu.VMEM(feed.shape, feed.dtype),
            pltpu.VMEM(grid.shape, grid.dtype),
            pltpu.VMEM((rows, L), jnp.bfloat16),
            pltpu.VMEM((rows // LANES, 2 * CH * PAIR, LANES), jnp.float32),
            pltpu.VMEM((blocks, 8, rows), jnp.bfloat16),
            pltpu.VMEM((blocks // 2, 8, rows), jnp.bfloat16),
            pltpu.VMEM((rows, (TAPS - 1) * L), jnp.bfloat16),
            pltpu.VMEM((frames, 2 * CH, rows), jnp.float32),
            pltpu.VMEM((frames, n_inp, CH // n_inp, rows), jnp.bfloat16),
            pltpu.VMEM((frames, n_inp, CH // n_inp, rows), jnp.bfloat16),
            pltpu.VMEM((rows, LANES), jnp.float32),
            pltpu.VMEM((inputs, LANES), jnp.int32),
            pltpu.VMEM((2, depth, inputs), jnp.bfloat16),
            pltpu.VMEM((2, depth, inputs), jnp.bfloat16),
            pltpu.VMEM((2, inputs, depth), jnp.bfloat16),
            pltpu.VMEM((2, inputs, depth), jnp.bfloat16),
            dma((chunks,)),
            dma((chunks,)),
            dma((chunks,)),
            dma((TAPS - 1,)),
            dma((TAPS - 1,)),
            dma((frames,)),
            dma((frames,)),
            dma((6,)),
        ],
        compiler_params=pltpu.CompilerParams(collective_id=0, has_side_effects=True, vmem_limit_bytes=30 << 20),
    )(*(pltpu.with_memory_space_constraint(a, pltpu.HBM) for a in (volt, gain, jnp.asarray(window_table()), jnp.asarray(dft_table(n_time, n_inp)), feed, grid)))


def products_kernel(n_time, n_inp, recv, cosine, sine, sums, part, visible, power, spec, turn, spec_t, turn_t):
    ch = pl.program_id(0)
    j = pl.program_id(1)

    @pl.when((ch == 0) & (j == 0))
    def _():
        arrange(recv, n_time * n_inp, n_time, n_inp, spec, turn, spec_t, turn_t)

    width = visible.shape[-1]
    cols = pl.ds(pl.multiple_of(j * width, width), width)
    right = spec[ch, :, cols]
    scale = 1.0 / (4 * n_time)
    for p, left in ((0, spec_t), (1, turn_t)):
        total = sums[ch, p, :, cols] + jnp.dot(left[ch], right, preferred_element_type=jnp.float32)
        visible[0, p] = (total * scale).astype(jnp.bfloat16)
    power[pl.ds(ch, 1), cols] = (part[ch, :, cols] + beam_sum(spec, turn, cosine, sine, ch, cols)) * scale


def products(recv, cosine, sine, sums, part, n_time, n_inp):
    inputs, beams = cosine.shape
    width = 512
    depth = n_time * 4
    vmem = pl.BlockSpec(memory_space=pltpu.VMEM)
    return pl.pallas_call(
        functools.partial(products_kernel, n_time, n_inp),
        name="products",
        grid=(2, inputs // width),
        out_shape=(
            jax.ShapeDtypeStruct((2, 2, inputs, inputs), jnp.bfloat16),
            jax.ShapeDtypeStruct((2, beams), jnp.float32),
        ),
        in_specs=[vmem] * 5,
        out_specs=(
            pl.BlockSpec((1, 2, inputs, width), lambda c, j: (c, 0, 0, j)),
            vmem,
        ),
        scratch_shapes=[
            pltpu.VMEM((2, depth, inputs), jnp.bfloat16),
            pltpu.VMEM((2, depth, inputs), jnp.bfloat16),
            pltpu.VMEM((2, inputs, depth), jnp.bfloat16),
            pltpu.VMEM((2, inputs, depth), jnp.bfloat16),
        ],
        compiler_params=pltpu.CompilerParams(vmem_limit_bytes=12 << 20),
    )(recv, cosine, sine, sums, part)


def on_device(voltages, input_gain, input_feed, beam_grid):
    n_time = lax.axis_size("tm")
    n_inp = lax.axis_size("inp")
    got = exchange(voltages, input_gain[None], input_feed[None], beam_grid[None], n_time, n_inp)
    return products(*got, n_time, n_inp)


def solution(mesh):
    return jax.shard_map(
        on_device,
        mesh=mesh,
        in_specs=(P("inp", "tm"), P("inp"), P(), P()),
        out_specs=(P(("tm", "inp"), None, None, None), P(("tm", "inp"), None)),
        check_vma=False,
    )
```
